128 devices in a mesh: band: 32 (over z, x, core), lev: 4 (over y).
Axes of the slice: x: 4, y: 4, z: 4, core: 2. Of those that a mesh axis runs over, the one named last changes fastest.
Arguments:
- air_fourier_coefficients: float32 [4, 16, 1280, 256], P('lev', None, 'band'), may hold values from -6 to 6
- quadrature_factor: float32 [1280], P('band'), may hold values from 0.5 to 1.5
- associated_polynomial_table: bfloat16 [128, 1280, 1280], P('band'), may hold values from -6 to 6
- east_west_harmonic: int32 [128], replicated, may hold values from 0 to 1279, as said below
- boundary_diffusion: float32 [4, 16, 16, 1280], P('lev', None, None, 'band'), may hold values from -0.25 to 0.25
- bulk_transfer_coefficient: float32 [4, 1280], P('lev', 'band'), may hold values from 0.1 to 1
- skin_heat_earlier: float32 [12, 4, 1280, 256], P(None, 'lev', 'band'), may hold values from -6 to 6
- sea_boundary_values: float32 [4, 1024, 1440], P('lev', 'band'), may hold values from -6 to 6
- sea_damping_speed: float32 [4, 1024, 1440], P('lev', 'band'), may hold values from 0.02 to 2
- sea_coupling_matrix: float32 [4, 4], replicated, may hold values from -1.75 to 1.75
- patch_active_entries: int32 [32], P('band'), may hold values from 8 to 32, as said below
- sea_southern_parallel: int32 [1024], P('band'), may hold values from 0 to 1278, as said below
- sea_northern_share: float32 [1024], P('band'), may hold values from 0 to 1
- air_paired_cells: int32 [2, 1280], P(None, 'band'), may hold values from 0 to 1023, as said below
- air_second_share: float32 [1280], P('band'), may hold values from 0 to 1
Outputs:
- air_coefficients_end: float32 [4, 16, 1280, 256], P('lev', None, 'band')
- sea_values_end: float32 [4, 1024, 1440], P('lev', 'band')
- skin_heat_newest: float32 [12, 4, 1280, 256], P(None, 'lev', 'band')
The draws below stay inside these ranges and needn't reach their ends.
Inputs may be any that keep to these rules, and one draw needn't show every extreme that they name: `east_west_harmonic`: Distinct; positions 2 j and 2 j + 1 hold m and 1279 - m for some m below 640; 0 is among them. `patch_active_entries`: the live slots of a tile come first; the last tile is full. For a slot of tile t, sea_southern_parallel and sea_southern_parallel + 1 lie in t * 40 - 8 to (t + 1) * 40 + 7; they do not decrease along a tile's live slots. `air_paired_cells`: for a latitude of band t both taps are live slots of tiles t - 1, t or t + 1, the first one of tile t, and the two differ.
All inputs are finite; a program needn't handle non-finite values.
Results may differ from the reference program's by a relative error of at most 0.014.
Values may be sent and summed in bfloat16 or wider, within the bound.
No kernel may reach another device: no remote copies, remote signals or barrier semaphores. Data moves between devices by JAX's collectives and lax.ppermute only.
A program may use at most 64 MiB of HBM per device.

```python
import math
import jax
import jax.numpy as jnp
from jax import lax

PARALLEL_NUMBER = 1280
NDEG = 1280
OLON = 1440
PROGNOSTIC_NUM = 4
LEVS = 16
SUBSTEP_NUMBER = 12
OROWS = 32
MARG = 8
HARMONIC_NUMBER = 128
LAT_DEV = 40
TILES = 32
OSLOTS = 1024


def rows_of_tiles(key):
    tile_key = jax.random.fold_in(key, 11)
    count_key, small_key = jax.random.split(tile_key)
    counts = jax.random.randint(count_key, (TILES,), OROWS // 4, OROWS + 1)
    smallest = jax.random.randint(small_key, (), 0, TILES - 1)
    tile_ids = jnp.arange(TILES)
    counts = jnp.where(tile_ids == smallest, OROWS // 4, counts)
    counts = jnp.where(tile_ids == TILES - 1, OROWS, counts)
    return counts.astype(jnp.int32)


def draw_patch_active_entries(key, part):
    return rows_of_tiles(key)


def draw_sea_southern_parallel(key, part):
    counts = rows_of_tiles(key)
    slot_index = jnp.arange(TILES * OROWS, dtype=jnp.int32)
    tile_index = slot_index // OROWS
    within = slot_index % OROWS
    count_here = counts[tile_index]
    within = jnp.minimum(within, count_here - 1)
    span_rows = LAT_DEV + 2 * MARG - 1
    lower = tile_index * LAT_DEV - MARG + within * span_rows // count_here
    lower = jnp.where((tile_index == TILES - 1) & (within == count_here - 1), PARALLEL_NUMBER - 2, lower)
    return jnp.clip(lower, 0, PARALLEL_NUMBER - 2).astype(jnp.int32)


def draw_air_paired_cells(key, part):
    counts = rows_of_tiles(key)
    latitude = jnp.arange(PARALLEL_NUMBER, dtype=jnp.int32)
    band_index = latitude // LAT_DEV
    within = latitude % LAT_DEV
    count_here = counts[band_index]
    first_slot = within * count_here // LAT_DEV
    first_cell_index = band_index * OROWS + first_slot
    next_slot = jnp.where(first_slot + 1 < count_here, first_slot + 1, first_slot - 1)
    before_ok = (within < MARG) & (band_index > 0)
    after_ok = (within >= LAT_DEV - MARG) & (band_index < TILES - 1) & jnp.logical_not(before_ok)
    count_before = counts[jnp.clip(band_index - 1, 0, TILES - 1)]
    closing_cell_index = jnp.where(before_ok, (band_index - 1) * OROWS + count_before - 1, jnp.where(after_ok, (band_index + 1) * OROWS, band_index * OROWS + next_slot))
    return jnp.stack([first_cell_index, closing_cell_index]).astype(jnp.int32)


def draw_east_west_harmonic(key, part):
    wave_key = jax.random.fold_in(key, 23)
    pick_key, order_key = jax.random.split(wave_key)
    half_count = NDEG // 2
    pair_count = HARMONIC_NUMBER // 2
    others = jax.random.permutation(pick_key, half_count - 1)[:pair_count - 1] + 1
    lowest = jnp.concatenate([jnp.zeros((1,), jnp.int32), others.astype(jnp.int32)])
    lowest = lowest[jax.random.permutation(order_key, pair_count)]
    paired = jnp.stack([lowest, NDEG - 1 - lowest], axis=1).reshape(HARMONIC_NUMBER)
    return paired.astype(jnp.int32)


def level_of(key, dims, shards, low, top_value):
    gain, own = 1.0, jax.random.fold_in(key, 6)
    for dim, shards_of in shards:
        steps = jnp.exp(jax.random.uniform(jax.random.fold_in(own, dim), (shards_of,), jnp.float32, low / len(shards), top_value / len(shards)))
        gain = gain * jnp.repeat(steps, dims[dim] // shards_of).reshape([-1 if axis == dim else 1 for axis in range(len(dims))])
    return gain


def gaussian(key, shape, spread, limit, pieces=(), kind=jnp.bfloat16):
    level = level_of(key, shape, pieces, -0.22, 0.18) if pieces else 1.0
    entries = jax.random.normal(key, shape, jnp.float32) * spread * level
    return jnp.minimum(jnp.maximum(entries, -limit), limit).astype(kind)


def setup_inputs(seed: int = 0) -> dict:
    streams_of = jax.random.split(jax.random.key(seed), 16)
    return {
        "air_fourier_coefficients": gaussian(streams_of[0], (PROGNOSTIC_NUM, LEVS, PARALLEL_NUMBER, 2 * HARMONIC_NUMBER), 1.0, 6.0, ((0, 4), (2, 32)), jnp.float32),
        "quadrature_factor": jnp.clip(0.5 + 1.0 * jax.random.uniform(streams_of[1], (PARALLEL_NUMBER,), jnp.float32) ** level_of(streams_of[1], (PARALLEL_NUMBER,), ((0, 32),), -0.2, 0.2), 0.5, 1.5),
        "associated_polynomial_table": gaussian(streams_of[2], (HARMONIC_NUMBER, PARALLEL_NUMBER, NDEG), 1.0, 6.0, ((0, 32),)),
        "east_west_harmonic": draw_east_west_harmonic(jax.random.fold_in(streams_of[15], 71), 0),
        "boundary_diffusion": gaussian(streams_of[4], (PROGNOSTIC_NUM, LEVS, LEVS, PARALLEL_NUMBER), 0.04, 0.25, ((0, 4), (3, 32)), jnp.float32),
        "bulk_transfer_coefficient": jnp.clip(jnp.exp(math.log(1.0) - 2.3025851 * jax.random.uniform(streams_of[5], (PROGNOSTIC_NUM, PARALLEL_NUMBER), jnp.float32) ** level_of(streams_of[5], (PROGNOSTIC_NUM, PARALLEL_NUMBER), ((0, 4), (1, 32)), -0.2, 0.2)), 0.1, 1.0),
        "skin_heat_earlier": gaussian(streams_of[6], (SUBSTEP_NUMBER, PROGNOSTIC_NUM, PARALLEL_NUMBER, 2 * HARMONIC_NUMBER), 1.0, 6.0, ((1, 4), (2, 32)), jnp.float32),
        "sea_boundary_values": gaussian(streams_of[7], (PROGNOSTIC_NUM, OSLOTS, OLON), 1.0, 6.0, ((0, 4), (1, 32)), jnp.float32),
        "sea_damping_speed": jnp.clip(jnp.exp(math.log(2.0) - 4.6051702 * jax.random.uniform(streams_of[8], (PROGNOSTIC_NUM, OSLOTS, OLON), jnp.float32) ** level_of(streams_of[8], (PROGNOSTIC_NUM, OSLOTS, OLON), ((0, 4), (1, 32)), -0.2, 0.2)), 0.02, 2.0),
        "sea_coupling_matrix": gaussian(streams_of[9], (PROGNOSTIC_NUM, PROGNOSTIC_NUM), 0.3, 1.75, (), jnp.float32),
        "patch_active_entries": draw_patch_active_entries(jax.random.fold_in(streams_of[15], 71), 0),
        "sea_southern_parallel": draw_sea_southern_parallel(jax.random.fold_in(streams_of[15], 71), 0),
        "sea_northern_share": jnp.clip(1.0 * jax.random.uniform(streams_of[12], (OSLOTS,), jnp.float32) ** level_of(streams_of[12], (OSLOTS,), ((0, 32),), -0.2, 0.2), 0.0, 1.0),
        "air_paired_cells": draw_air_paired_cells(jax.random.fold_in(streams_of[15], 71), 0),
        "air_second_share": jnp.clip(1.0 * jax.random.uniform(streams_of[14], (PARALLEL_NUMBER,), jnp.float32) ** level_of(streams_of[14], (PARALLEL_NUMBER,), ((0, 32),), -0.2, 0.2), 0.0, 1.0),
    }


degree_damping = 2e-06
ocean_step = 0.5
mixing_diagonal = 0.95
synth_divisor = 4.0

def damping_table(wave_values):
    degrees = wave_values[:, None] + jnp.arange(NDEG, dtype=jnp.int32)[None, :]
    degree_float = degrees.astype(jnp.float32)
    factor = 1.0 / (1.0 + degree_damping * degree_float * (degree_float + 1.0))
    return jnp.where(degrees < NDEG, factor, jnp.zeros_like(factor))

def zonal_table(wave_values):
    longitude = jnp.arange(OLON, dtype=jnp.int32)
    phases = wave_values[:, None] * longitude[None, :] % OLON
    angles = phases.astype(jnp.float32) * (2.0 * math.pi / OLON)
    stacked = jnp.stack([jnp.cos(angles), -jnp.sin(angles)], axis=1)
    return stacked.reshape(2 * wave_values.shape[0], OLON).astype(jnp.bfloat16)

def mixing_matrix(boundary_diffusion):
    level_count = boundary_diffusion.shape[1]
    identity_block = jnp.eye(level_count, dtype=jnp.float32)[None, :, :, None]
    return mixing_diagonal * identity_block + boundary_diffusion - jnp.transpose(boundary_diffusion, (0, 2, 1, 3))

def legendre_pair(inputs):
    values, table, damping = inputs
    spectral = jnp.einsum('rlc,ln->rnc', values.astype(jnp.float32), table.astype(jnp.float32))
    damped = (spectral * damping[None, :, None]).astype(jnp.bfloat16)
    synthesis = jnp.einsum('rnc,ln->rlc', damped.astype(jnp.float32), table.astype(jnp.float32))
    synthesis = synthesis * (1.0 / (synth_divisor * math.sqrt(NDEG)))
    return synthesis.astype(jnp.bfloat16)

def reference(air_fourier_coefficients, quadrature_factor, associated_polynomial_table, east_west_harmonic, boundary_diffusion, bulk_transfer_coefficient, skin_heat_earlier, sea_boundary_values, sea_damping_speed, sea_coupling_matrix, patch_active_entries, sea_southern_parallel, sea_northern_share, air_paired_cells, air_second_share):
    fields = air_fourier_coefficients.shape[0]
    height_pile = air_fourier_coefficients.shape[1]
    row_count = fields * height_pile
    damping = damping_table(east_west_harmonic)
    mixing = mixing_matrix(boundary_diffusion)
    weight = quadrature_factor * (1.0 / math.sqrt(PARALLEL_NUMBER))

    def march_air_model(air_model_present, skin_heat_present):
        scaled = (air_model_present * weight[None, None, :, None]).astype(jnp.bfloat16)
        columns = scaled.reshape(row_count, PARALLEL_NUMBER, HARMONIC_NUMBER, 2).transpose(2, 0, 1, 3)
        synthesis = lax.map(legendre_pair, (columns, associated_polynomial_table, damping))
        synthesis = synthesis.transpose(1, 2, 0, 3).reshape(fields, height_pile, PARALLEL_NUMBER, 2 * HARMONIC_NUMBER).astype(jnp.float32)
        halfway_point = air_model_present - synthesis
        bottom_sheet = bulk_transfer_coefficient[:, :, None] * (skin_heat_present - halfway_point[:, height_pile - 1])
        mixed_state = jnp.einsum('flpa,fpac->flac', mixing, halfway_point, precision=lax.Precision.HIGHEST)
        mixed_state = mixed_state.at[:, height_pile - 1].add(bottom_sheet)
        return (mixed_state, bottom_sheet.astype(jnp.bfloat16))
    air_coefficients_end, forcing_series = lax.scan(march_air_model, air_fourier_coefficients, skin_heat_earlier)
    slot_index = jnp.arange(OSLOTS, dtype=jnp.int32)
    live_slot = slot_index % OROWS < patch_active_entries[slot_index // OROWS]
    low_tap = jnp.where(live_slot, 1.0 - sea_northern_share, jnp.zeros_like(sea_northern_share)).astype(jnp.bfloat16)
    high_tap = jnp.where(live_slot, sea_northern_share, jnp.zeros_like(sea_northern_share)).astype(jnp.bfloat16)
    lower_rows = jnp.take(forcing_series, sea_southern_parallel, axis=2).astype(jnp.float32)
    upper_rows = jnp.take(forcing_series, sea_southern_parallel + 1, axis=2).astype(jnp.float32)
    ocean_flux = (low_tap.astype(jnp.float32)[None, None, :, None] * lower_rows + high_tap.astype(jnp.float32)[None, None, :, None] * upper_rows).astype(jnp.bfloat16)
    zonal_basis = zonal_table(east_west_harmonic).astype(jnp.float32)
    synth_scale = 1.0 / math.sqrt(2 * HARMONIC_NUMBER)
    skew_coupling = sea_coupling_matrix - sea_coupling_matrix.T

    def ocean_advance(ocean_now, flux_now):
        forcing = jnp.einsum('fsc,cx->fsx', flux_now.astype(jnp.float32), zonal_basis) * synth_scale
        coarse = lax.optimization_barrier(ocean_now.astype(jnp.bfloat16)).astype(jnp.float32)
        coupled = jnp.einsum('fe,esx->fsx', skew_coupling, coarse, precision=lax.Precision.HIGHEST)
        updated = (ocean_now + ocean_step * (coupled - forcing)) / (1.0 + ocean_step * sea_damping_speed)
        return (updated, updated.astype(jnp.bfloat16))
    sea_values_end, ocean_wave = lax.scan(ocean_advance, sea_boundary_values, ocean_flux)

    def analyse(wave_now):
        coef = jnp.einsum('fsx,cx->fsc', wave_now.astype(jnp.float32), zonal_basis) * (1.0 / math.sqrt(OLON))
        return coef.astype(jnp.bfloat16)
    ocean_coef = lax.map(analyse, ocean_wave)
    first_cell_index = (1.0 - air_second_share).astype(jnp.bfloat16).astype(jnp.float32)
    closing_cell_index = air_second_share.astype(jnp.bfloat16).astype(jnp.float32)
    first_band_entries = jnp.take(ocean_coef, air_paired_cells[0], axis=2).astype(jnp.float32)
    final_band_entries = jnp.take(ocean_coef, air_paired_cells[1], axis=2).astype(jnp.float32)
    skin_heat_newest = first_cell_index[None, None, :, None] * first_band_entries + closing_cell_index[None, None, :, None] * final_band_entries
    return (air_coefficients_end, sea_values_end, skin_heat_newest)
```

```python
import math

import jax
import jax.numpy as jnp
import numpy as np
from jax import lax
from jax.experimental import pallas as pl
from jax.experimental.pallas import tpu as pltpu
from jax.sharding import PartitionSpec as P

MARG = 8
AXES = ("band", "lev")
degree_damping = 2e-06
ocean_step = 0.5
mixing_diagonal = 0.95
synth_divisor = 4.0

BANDS, FIELDS = 32, 4
LEVELS, LAT, COLS = 16, 40, 256
NLAT = BANDS * LAT
WAVES = COLS // 2
STEPS = 12
SLOTS = 32
HALF = LAT // 2
ITEMS = 32
PAIRS = [(l, p) for l in range(LEVELS) for p in range(l + 1, LEVELS)]
NPAIR = len(PAIRS)
XROWS = 24
CHUNK = XROWS + LAT
BF = jnp.bfloat16
F32 = jnp.float32
NT = (((1,), (1,)), ((), ()))


def pair_matrix():
    q = np.zeros((LEVELS * LEVELS, 128), np.float32)
    for i, (l, p) in enumerate(PAIRS):
        q[l * LEVELS + p, i] = 1.0
        q[p * LEVELS + l, i] = -1.0
    return q


def damping_table(wave_values, degree_count):
    degrees = wave_values[:, None] + jnp.arange(degree_count, dtype=jnp.int32)[None, :]
    degree_float = degrees.astype(F32)
    factor = 1.0 / (1.0 + degree_damping * degree_float * (degree_float + 1.0))
    return jnp.where(degrees < degree_count, factor, jnp.zeros_like(factor))


def hi_lo(v):
    hi = lax.reduce_precision(v, 8, 7)
    return hi, v - hi


def pack_kernel(x_ref, s_ref, e_ref, m_ref, o_ref, d_ref, t_ref):
    row = lax.broadcasted_iota(jnp.int32, (COLS, COLS), 0)
    col = lax.broadcasted_iota(jnp.int32, (COLS, COLS), 1)
    spread = jnp.where(row == 2 * (col % WAVES) + col // WAVES, 1.0, 0.0).astype(BF)
    base = 0
    for ref in (x_ref, s_ref, e_ref):
        n = ref.shape[0]
        d = jnp.dot(ref[...].astype(BF), spread, preferred_element_type=F32)
        d_ref[0, base : base + n, :] = d[:, :WAVES]
        d_ref[1, base : base + n, :] = d[:, WAVES:]
        base += n
    for h in range(HALF):
        parts = [
            d_ref[c, pl.ds(lo * HALF + h, ITEMS, stride=LAT), :] for c in range(2) for lo in range(2)
        ]
        t_ref[pl.ds(h, WAVES, stride=XROWS), :] = jnp.concatenate(parts, axis=0).T
    mix = m_ref[...]

    def put(m, _):
        o_ref[m, 0:XROWS, :] = t_ref[pl.ds(pl.multiple_of(m * XROWS, 8), XROWS), :].astype(BF)
        o_ref[m, XROWS:CHUNK, :] = mix
        return 0

    for h in range(HALF, XROWS):
        t_ref[pl.ds(h, WAVES, stride=XROWS), :] = jnp.zeros((WAVES, 128), F32)
    lax.fori_loop(0, WAVES, put, 0)


def atmosphere_kernel(rm_ref, rx_ref, sm_ref, sx_ref, p_ref, g_ref, xo_ref, fo_ref, a_ref, x_ref, y_ref, f_ref):
    for n in range(NLAT // 256):
        a_ref[:, n * 256 : (n + 1) * 256] = lax.dot_general(
            sm_ref[...], rm_ref[n * 256 : (n + 1) * 256, :], NT, preferred_element_type=F32
        )
    for lo in range(2):
        x_ref[:, lo * 640 : (lo + 1) * 640] = lax.dot_general(
            sx_ref[lo], rx_ref[...], NT, preferred_element_type=F32
        )

    def step(k, _):
        weight = x_ref[28 * 8 : 29 * 8, :]
        state = x_ref[0:128, :].reshape(LEVELS, 8, NLAT) * weight[None]
        y_ref[...] = jnp.dot(
            state.reshape(128, NLAT).astype(BF), p_ref[...], preferred_element_type=F32
        )

        def block(n, _):
            lanes = pl.ds(pl.multiple_of(n * 128, 128), 128)
            mid = [
                x_ref[8 * l : 8 * l + 8, lanes] - y_ref[8 * l : 8 * l + 8, lanes]
                for l in range(LEVELS)
            ]
            skin = x_ref[pl.ds(pl.multiple_of(128 + 8 * k, 8), 8), lanes]
            flux = x_ref[29 * 8 : 30 * 8, lanes] * (skin - mid[LEVELS - 1])
            f_ref[pl.ds(pl.multiple_of(8 * k, 8), 8), lanes] = flux
            acc = [mixing_diagonal * v for v in mid]
            acc[LEVELS - 1] = acc[LEVELS - 1] + flux
            for i, (l, p) in enumerate(PAIRS):
                a = a_ref[8 * i : 8 * i + 8, lanes]
                acc[l] = acc[l] + a * mid[p]
                acc[p] = acc[p] - a * mid[l]
            for l in range(LEVELS):
                x_ref[8 * l : 8 * l + 8, lanes] = acc[l]
            return 0

        lax.fori_loop(0, NLAT // 128, block, 0)
        return 0

    lax.fori_loop(0, STEPS, step, 0)
    xo_ref[...] = x_ref[0:128, :].astype(BF)
    fo_ref[...] = jnp.dot(f_ref[...].astype(BF), g_ref[...], preferred_element_type=F32).astype(BF)


def ocean_kernel(lev_ref, f_ref, zt_ref, z_ref, c_ref, o0_ref, r_ref, so_ref, co_ref, o_ref, t_ref):
    o_ref[...] = o0_ref[...]
    start = pl.multiple_of(lev_ref[0] * SLOTS, SLOTS)
    scale = 1.0 / math.sqrt(z_ref.shape[1])

    def step(k, _):
        ocean = o_ref[...]
        coarse = ocean.astype(BF)
        push = jnp.dot(zt_ref[...], f_ref[k], preferred_element_type=F32)
        pull = jnp.dot(coarse, c_ref[0], preferred_element_type=F32)
        pull = pull + jnp.dot(coarse, c_ref[1], preferred_element_type=F32)
        updated = (ocean + (pull + push)) * r_ref[...]
        o_ref[...] = updated
        coef = jnp.dot(z_ref[...], updated.astype(BF), preferred_element_type=F32) * scale
        t_ref[...] = coef.T
        co_ref[k] = t_ref[pl.ds(start, SLOTS), :].astype(BF)
        return 0

    lax.fori_loop(0, STEPS, step, 0)
    lon = o_ref.shape[0]
    for x in range(0, lon, 128):
        w = min(128, lon - x)
        t_ref[:, 0:w] = o_ref[x : x + w, :].T
        so_ref[:, x : x + w] = t_ref[pl.ds(start, SLOTS), 0:w]


def vmem(n):
    return [pl.BlockSpec(memory_space=pltpu.VMEM)] * n


def per_device(
    air_fourier_coefficients,
    quadrature_factor,
    associated_polynomial_table,
    east_west_harmonic,
    boundary_diffusion,
    bulk_transfer_coefficient,
    skin_heat_earlier,
    sea_boundary_values,
    sea_damping_speed,
    sea_coupling_matrix,
    patch_active_entries,
    sea_southern_parallel,
    sea_northern_share,
    air_paired_cells,
    air_second_share,
):
    band = lax.axis_index("band")
    lev = lax.axis_index("lev")
    lon = sea_boundary_values.shape[2]
    degree_count = associated_polynomial_table.shape[2]

    w_hi, w_lo = hi_lo(quadrature_factor)
    b_hi, b_lo = hi_lo(bulk_transfer_coefficient[0])
    live = jnp.arange(SLOTS, dtype=jnp.int32) < patch_active_entries[0]
    offset = (sea_southern_parallel - (band * LAT - MARG)).astype(F32)
    low = jnp.where(live, 1.0 - sea_northern_share, 0.0)
    high = jnp.where(live, sea_northern_share, 0.0)
    taps = jnp.where(lev == 0, offset, jnp.where(lev == 1, low, high))
    taps = jnp.pad(taps, (0, LAT - SLOTS))
    even = (jnp.arange(COLS) % 2 == 0)[None, :]
    extra = jnp.concatenate(
        [
            jnp.where(even, w_hi[:, None], w_lo[:, None]),
            jnp.where(even, b_hi[:, None], b_lo[:, None]),
            jnp.broadcast_to(taps[:, None], (LAT, COLS)),
            jnp.zeros((LAT, COLS), F32),
        ],
        axis=0,
    )
    mix = jnp.einsum(
        "rg,ri->gi",
        boundary_diffusion.reshape(LEVELS * LEVELS, LAT),
        jnp.asarray(pair_matrix()),
        precision=lax.Precision.HIGHEST,
    ).astype(BF)
    chunks = pl.pallas_call(
        pack_kernel,
        out_shape=jax.ShapeDtypeStruct((WAVES, CHUNK, 128), BF),
        in_specs=vmem(4),
        out_specs=pl.BlockSpec(memory_space=pltpu.VMEM),
        scratch_shapes=[
            pltpu.VMEM((2, ITEMS * LAT, 128), F32),
            pltpu.VMEM((WAVES * XROWS, 128), F32),
        ],
        name="pack_in",
    )(
        air_fourier_coefficients.reshape(LEVELS * LAT, COLS),
        skin_heat_earlier.reshape(STEPS * LAT, COLS),
        extra,
        mix,
    )
    got = lax.all_to_all(chunks, AXES, 0, 0, tiled=True)

    table = lax.dynamic_index_in_dim(associated_polynomial_table, lev, 0, keepdims=False)
    table = table.reshape(BANDS, 2, HALF, degree_count).transpose(1, 0, 2, 3).reshape(NLAT, degree_count)
    wave = lax.dynamic_slice_in_dim(east_west_harmonic, band * FIELDS + lev, 1, 0)
    damping = damping_table(wave, degree_count)
    damped = (table * damping).astype(BF)
    operator = lax.dot_general(table, damped, NT, preferred_element_type=F32)
    operator = (operator * (1.0 / (synth_divisor * math.sqrt(degree_count) * math.sqrt(NLAT)))).astype(BF)

    row = jnp.arange(NPAIR * 8, dtype=jnp.int32)[:, None]
    col = jnp.arange(FIELDS * 128, dtype=jnp.int32)[None, :]
    select_mix = ((row // 8 == col % 128) & (row % 8 // 2 == col // 128)).astype(BF)
    row = jnp.arange(ITEMS * 8, dtype=jnp.int32)[:, None]
    item = row // 8
    same = (col % ITEMS == item) & (col // 128 == row % 8 // 2)
    same_c = (col % 128 // 64 == row % 2) | (item == 28) | (item == 29)
    select_x = jnp.stack([same & same_c & (col % 64 // ITEMS == lo) for lo in range(2)]).astype(BF)

    longitude = jnp.arange(lon, dtype=jnp.int32)
    phases = east_west_harmonic[:, None] * longitude[None, :] % lon
    angles = phases.astype(F32) * (2.0 * math.pi / lon)
    cosine, sine = jnp.cos(angles).astype(BF), (-jnp.sin(angles)).astype(BF)
    zonal = jnp.stack([cosine, sine], axis=1).reshape(COLS, lon)
    push_scale = -ocean_step / math.sqrt(COLS)
    zonal_t = (jnp.concatenate([cosine, sine], axis=0).astype(F32) * push_scale).astype(BF).T
    own = jnp.concatenate([sea_boundary_values[0], sea_damping_speed[0]], axis=0)
    sent = own.astype(BF)
    shifted = [sent]
    for d in range(1, FIELDS):
        shifted.append(lax.ppermute(sent, "lev", [(i, (i + d) % FIELDS) for i in range(FIELDS)]))
    shifted = jnp.stack(shifted)
    fields = []
    for f in range(FIELDS):
        other = lax.dynamic_index_in_dim(shifted, (lev - f) % FIELDS, 0, keepdims=False)
        fields.append(jnp.where(lev == f, own, other.astype(F32)))
    fields = jnp.stack(fields).reshape(FIELDS, 2, SLOTS, lon)
    ocean0 = fields[:, 0].reshape(FIELDS * SLOTS, lon).T
    shrink = 1.0 / (1.0 + ocean_step * fields[:, 1].reshape(FIELDS * SLOTS, lon).T)
    skew = ocean_step * (sea_coupling_matrix - sea_coupling_matrix.T)
    couple = jnp.kron(skew.T, jnp.eye(SLOTS, dtype=F32))
    couple = jnp.stack(hi_lo(couple)).astype(BF)

    gotx = got[:, :HALF].reshape(BANDS, FIELDS, HALF, 128)
    recv_x = gotx.transpose(0, 2, 1, 3).reshape(BANDS * HALF, FIELDS * 128)
    recv_m = (
        got[:, XROWS:].reshape(BANDS, FIELDS, 2, HALF, 128).transpose(2, 0, 3, 1, 4).reshape(NLAT, FIELDS * 128)
    )
    tap = gotx.reshape(BANDS, FIELDS, HALF, 2, 2, ITEMS)[:, :3, :, 0, :, 30]
    tap = tap.transpose(1, 0, 3, 2).reshape(3, BANDS, LAT)[:, :, :SLOTS].astype(F32).reshape(3, 1, BANDS * SLOTS)
    south = tap[0] + (jnp.arange(BANDS * SLOTS, dtype=jnp.int32) // SLOTS * LAT - MARG).astype(F32)[None]
    place = jnp.arange(NLAT, dtype=jnp.int32)
    place = place % 640 // HALF * LAT + place // 640 * HALF + place % HALF
    place = place.astype(F32)[:, None]
    to_slots = (jnp.where(place == south, tap[1], 0.0) + jnp.where(place == south + 1.0, tap[2], 0.0)).astype(BF)

    air_end, slot_flux = pl.pallas_call(
        atmosphere_kernel,
        out_shape=(
            jax.ShapeDtypeStruct((128, NLAT), BF),
            jax.ShapeDtypeStruct((STEPS * 8, BANDS * SLOTS), BF),
        ),
        in_specs=vmem(6),
        out_specs=tuple(vmem(2)),
        scratch_shapes=[
            pltpu.VMEM((NPAIR * 8, NLAT), F32),
            pltpu.VMEM((ITEMS * 8, NLAT), F32),
            pltpu.VMEM((128, NLAT), F32),
            pltpu.VMEM((STEPS * 8, NLAT), F32),
        ],
        name="atmosphere",
    )(recv_m, recv_x, select_mix, select_x, operator, to_slots)

    flux_out = slot_flux.reshape(STEPS, FIELDS, 2, BANDS, SLOTS).transpose(3, 2, 0, 1, 4)
    flux_out = jnp.broadcast_to(
        flux_out.reshape(BANDS, 1, 2 * STEPS, 128), (BANDS, FIELDS, 2 * STEPS, 128)
    ).reshape(WAVES, 2 * STEPS, 128)
    air_out = air_end.reshape(LEVELS, FIELDS, 2, 2, BANDS, HALF).transpose(4, 1, 2, 0, 3, 5)
    air_out = air_out.reshape(WAVES, 10, 128)
    out = jnp.concatenate([flux_out, air_out, jnp.zeros((WAVES, 6, 128), BF)], axis=1)
    back = lax.all_to_all(out, AXES, 0, 0, tiled=True)
    air_coefficients_end = (
        back[:, 24:34].reshape(COLS, LEVELS * LAT).T.astype(F32).reshape(1, LEVELS, LAT, COLS)
    )
    flux_in = back[:, :24].reshape(WAVES, 2, STEPS, 128).transpose(2, 1, 0, 3).reshape(STEPS, COLS, 128)

    sea_end, ocean_coef = pl.pallas_call(
        ocean_kernel,
        out_shape=(
            jax.ShapeDtypeStruct((SLOTS, lon), F32),
            jax.ShapeDtypeStruct((STEPS, SLOTS, COLS), BF),
        ),
        in_specs=[pl.BlockSpec(memory_space=pltpu.SMEM)] + vmem(6),
        out_specs=tuple(vmem(2)),
        scratch_shapes=[pltpu.VMEM((lon, 128), F32), pltpu.VMEM((128, COLS), F32)],
        name="ocean",
    )(lev.astype(jnp.int32)[None], flux_in, zonal_t, zonal, couple, ocean0, shrink)

    up = [(i, i + 1) for i in range(BANDS - 1)]
    down = [(j, i) for i, j in up]
    before = lax.ppermute(ocean_coef, "band", up)
    after = lax.ppermute(ocean_coef, "band", down)
    neighbours = jnp.concatenate([before, ocean_coef, after], axis=1)
    slot_index = jnp.arange(3 * SLOTS, dtype=jnp.int32)[None, :]
    first = (air_paired_cells[0] - (band - 1) * SLOTS)[:, None]
    second = (air_paired_cells[1] - (band - 1) * SLOTS)[:, None]
    return_taps = jnp.where(slot_index == first, (1.0 - air_second_share)[:, None], 0.0) + jnp.where(
        slot_index == second, air_second_share[:, None], 0.0
    )
    skin_heat_newest = jnp.einsum(
        "ga,kac->kgc", return_taps.astype(BF), neighbours, preferred_element_type=F32
    )[:, None]
    return (air_coefficients_end, sea_end[None], skin_heat_newest)


def solution(mesh):
    return jax.shard_map(
        per_device,
        mesh=mesh,
        in_specs=(
            P("lev", None, "band", None),
            P("band"),
            P("band", None, None),
            P(),
            P("lev", None, None, "band"),
            P("lev", "band"),
            P(None, "lev", "band", None),
            P("lev", "band", None),
            P("lev", "band", None),
            P(),
            P("band"),
            P("band"),
            P("band"),
            P(None, "band"),
            P("band"),
        ),
        out_specs=(
            P("lev", None, "band", None),
            P("lev", "band", None),
            P(None, "lev", "band", None),
        ),
        check_vma=False,
    )
```

```python
import math

import jax
import jax.numpy as jnp
import numpy as np
from jax import lax
from jax.experimental import pallas as pl
from jax.experimental.pallas import tpu as pltpu
from jax.sharding import PartitionSpec as P


MARG = 8
AXES = ("band", "lev")
degree_damping = 2e-06
ocean_step = 0.5
mixing_diagonal = 0.95
synth_divisor = 4.0

BANDS, FIELDS = 32, 4
LEVELS, LAT, COLS = 16, 40, 256
NLAT = BANDS * LAT
WAVES = COLS // 2
STEPS = 12
SLOTS = 32
LO = LAT // 8
ITEMS = 32
PAIRS = [(l, p) for l in range(LEVELS) for p in range(l + 1, LEVELS)]
NPAIR = len(PAIRS)
XROWS = 24
OUT_ROWS = 40
CHUNK = XROWS + LAT
BF = jnp.bfloat16
F32 = jnp.float32
NT = (((1,), (1,)), ((), ()))


def pair_matrix():
    q = np.zeros((LEVELS * LEVELS, 128), np.float32)
    for i, (l, p) in enumerate(PAIRS):
        q[l * LEVELS + p, i] = 1.0
        q[p * LEVELS + l, i] = -1.0
    return q


def hi_lo(v):
    hi = v.astype(BF)
    return hi, (v - hi.astype(F32)).astype(BF)


def split_columns():
    row = lax.broadcasted_iota(jnp.int32, (COLS, COLS), 0)
    col = lax.broadcasted_iota(jnp.int32, (COLS, COLS), 1)
    return jnp.where(row == 2 * (col % WAVES) + col // WAVES, 1.0, 0.0).astype(BF)


def join_columns():
    row = lax.broadcasted_iota(jnp.int32, (COLS, COLS), 0)
    col = lax.broadcasted_iota(jnp.int32, (COLS, COLS), 1)
    return jnp.where(col == 2 * (row % WAVES) + row // WAVES, 1.0, 0.0).astype(BF)


def block_transpose(arrays, width):
    arrays = list(arrays)
    block = lax.broadcasted_iota(jnp.int32, arrays[0].shape, 1) // width
    s = 1
    while s < len(arrays):
        upper = (block & s) != 0
        for i in range(len(arrays)):
            if not i & s:
                a, b = arrays[i], arrays[i | s]
                arrays[i] = jnp.where(upper, pltpu.roll(b, s * width, 1), a)
                arrays[i | s] = jnp.where(upper, b, pltpu.roll(a, 128 - s * width, 1))
        s *= 2
    return arrays


def pack_kernel(ids, live_ref, x_ref, s_ref, b_ref, w_ref, k_ref, south_ref, north_ref, q_ref, o_ref, d_ref, t_ref):
    spread = split_columns()
    base = 0
    for ref in (x_ref, s_ref):
        n = ref.shape[0]
        d = jnp.dot(ref[...].astype(BF), spread, preferred_element_type=F32)
        d_ref[0, base : base + n, :] = d[:, :WAVES]
        d_ref[1, base : base + n, :] = d[:, WAVES:]
        base += n
    slot = lax.broadcasted_iota(jnp.int32, (1, SLOTS), 1)
    live = slot < live_ref[0]
    offset = (south_ref[...] - (ids[0] * LAT - MARG)).astype(F32)
    low = jnp.where(live, 1.0 - north_ref[...], 0.0)
    high = jnp.where(live, north_ref[...], 0.0)
    kind = jnp.full((1, SLOTS), ids[1], jnp.int32)
    taps = jnp.where(kind == 0, offset, jnp.where(kind == 1, low, high))
    taps = jnp.concatenate([taps, jnp.zeros((1, LAT - SLOTS), F32)], axis=1)
    w_hi, w_lo = hi_lo(w_ref[...])
    k_hi, k_lo = hi_lo(k_ref[...])
    rows = [w_hi.astype(F32), w_lo.astype(F32), k_hi.astype(F32), k_lo.astype(F32), taps]
    small = jnp.concatenate(rows + [jnp.zeros((3, LAT), F32)], axis=0).T
    for c in range(2):
        for i, pick in enumerate((c, 2 + c, 4)):
            d_ref[c, (28 + i) * LAT : (29 + i) * LAT, :] = jnp.broadcast_to(
                small[:, pick : pick + 1], (LAT, WAVES)
            )
        d_ref[c, 31 * LAT : 32 * LAT, :] = jnp.zeros((LAT, WAVES), F32)
    m_hi, m_lo = hi_lo(b_ref[...].T)
    mix = jnp.dot(m_hi, q_ref[...], preferred_element_type=F32)
    mix = (mix + jnp.dot(m_lo, q_ref[...], preferred_element_type=F32)).astype(BF)
    for j in range(XROWS // 8):
        for h in range(8):
            parts = []
            for q in range(2):
                for c in range(2):
                    lo = 2 * j + q
                    if lo < LO:
                        parts.append(d_ref[c, pl.ds(lo * 8 + h, ITEMS, stride=LAT), :])
                    else:
                        parts.append(jnp.zeros((ITEMS, WAVES), F32))
            t_ref[pl.ds(j * 8 + h, WAVES, stride=XROWS), :] = jnp.concatenate(parts, axis=0).T

    def put(m, _):
        o_ref[m, 0:XROWS, :] = t_ref[pl.ds(pl.multiple_of(m * XROWS, 8), XROWS), :].astype(BF)
        o_ref[m, XROWS:CHUNK, :] = mix
        return 0

    lax.fori_loop(0, WAVES, put, 0)


def operator_kernel(ids, wave_ref, table_ref, p_ref, t_ref, d_ref, sem):
    def copy(lo):
        return pltpu.make_async_copy(table_ref.at[ids[1], :, lo], t_ref.at[lo], sem.at[lo])

    for lo in range(LO):
        copy(lo).start()
    degree_count = p_ref.shape[1]
    wave = wave_ref[ids[0] * FIELDS + ids[1]]
    degrees = wave + lax.broadcasted_iota(jnp.int32, (1, degree_count), 1)
    degree_float = degrees.astype(F32)
    damping = 1.0 / (1.0 + degree_damping * degree_float * (degree_float + 1.0))
    damping = jnp.where(degrees < degree_count, damping, 0.0)
    scale = 1.0 / (synth_divisor * math.sqrt(degree_count) * math.sqrt(NLAT))
    for lo in range(LO):
        copy(lo).wait()
        part = t_ref[lo].reshape(BANDS * 8, degree_count)
        d_ref[lo * 256 : (lo + 1) * 256, :] = (part.astype(F32) * damping).astype(BF)
    for lo in range(LO):
        part = t_ref[lo].reshape(BANDS * 8, degree_count)
        p = lax.dot_general(part, d_ref[...], NT, preferred_element_type=F32)
        p_ref[lo * 256 : (lo + 1) * 256, :] = (p * scale).astype(BF)


def tables_kernel(ids, c_ref, a_ref, own_s, own_d, o1, o2, o3, zt_ref, z_ref, so_ref, sr_ref, cp_ref, w_ref, h_ref):
    lon = own_s.shape[1]
    fine = a_ref[0:80, :]
    for q in range(lon // 40):
        ca = a_ref[80 + q : 81 + q, :]
        sa = a_ref[120 + q : 121 + q, :]
        cos = ca * fine[0:40] - sa * fine[40:80]
        sin = sa * fine[0:40] + ca * fine[40:80]
        w_ref[40 * q : 40 * q + 40, 0:WAVES] = cos
        w_ref[40 * q : 40 * q + 40, WAVES:COLS] = -sin
    zt_ref[...] = w_ref[...].astype(BF)
    for x in range(0, lon, 128):
        w = min(128, lon - x)
        for c in range(2):
            z_ref[c * WAVES : (c + 1) * WAVES, x : x + w] = (
                w_ref[x : x + w, c * WAVES : (c + 1) * WAVES].T.astype(BF)
            )
    for j, (sea, damp) in enumerate(
        [(own_s[...], own_d[...])] + [(o[0:SLOTS, :], o[SLOTS:, :]) for o in (o1, o2, o3)]
    ):
        field = (ids[1] + FIELDS - j) % FIELDS
        at = pl.multiple_of(field * SLOTS, SLOTS)
        h_ref[0, pl.ds(at, SLOTS), :] = sea.astype(F32)
        h_ref[1, pl.ds(at, SLOTS), :] = damp.astype(F32)
    for x in range(0, lon, 128):
        w = min(128, lon - x)
        so_ref[x : x + w, :] = h_ref[0, :, x : x + w].T
        sr_ref[x : x + w, :] = 1.0 / (1.0 + ocean_step * h_ref[1, :, x : x + w].T)
    row = lax.broadcasted_iota(jnp.int32, (128, 128), 0)
    col = lax.broadcasted_iota(jnp.int32, (128, 128), 1)
    same = row % SLOTS == col % SLOTS
    couple = jnp.zeros((128, 128), F32)
    for e in range(FIELDS):
        for f in range(FIELDS):
            v = ocean_step * (c_ref[f, e] - c_ref[e, f])
            couple = jnp.where(same & (row // SLOTS == e) & (col // SLOTS == f), v, couple)
    hi, lo = hi_lo(couple)
    cp_ref[0:128, :] = hi
    cp_ref[128:256, :] = lo


def atmosphere_kernel(
    g_ref, sm_ref, sx_ref, se_ref, p_ref, o_ref, a_ref, x_ref, y_ref, f_ref, t_ref
):
    for lo in range(LO):
        lanes = slice(lo * 256, (lo + 1) * 256)
        mix = jnp.concatenate([g_ref[f, 3 + lo] for f in range(FIELDS)], axis=1)
        a_ref[:, lanes] = lax.dot_general(sm_ref[...], mix, NT, preferred_element_type=F32)
        rows = jnp.concatenate([g_ref[f, lo // 2] for f in range(FIELDS)], axis=1)
        x_ref[:, lanes] = lax.dot_general(sx_ref[lo % 2], rows, NT, preferred_element_type=F32)

    def step(k, _):
        weight = x_ref[28 * 8 : 29 * 8, :]
        state = x_ref[0:128, :].reshape(LEVELS, 8, NLAT) * weight[None]
        y_ref[...] = jnp.dot(
            state.reshape(128, NLAT).astype(BF), p_ref[...], preferred_element_type=F32
        )

        def block(n, _):
            lanes = pl.ds(pl.multiple_of(n * 128, 128), 128)
            mid = [
                x_ref[8 * l : 8 * l + 8, lanes] - y_ref[8 * l : 8 * l + 8, lanes]
                for l in range(LEVELS)
            ]
            skin = x_ref[pl.ds(pl.multiple_of(128 + 8 * k, 8), 8), lanes]
            flux = x_ref[29 * 8 : 30 * 8, lanes] * (skin - mid[LEVELS - 1])
            f_ref[n, pl.ds(k, 8, stride=STEPS), :] = flux
            acc = [mixing_diagonal * v for v in mid]
            acc[LEVELS - 1] = acc[LEVELS - 1] + flux
            for i, (l, p) in enumerate(PAIRS):
                a = a_ref[8 * i : 8 * i + 8, lanes]
                acc[l] = acc[l] + a * mid[p]
                acc[p] = acc[p] - a * mid[l]
            for l in range(LEVELS):
                x_ref[8 * l : 8 * l + 8, lanes] = acc[l]
            return 0

        lax.fori_loop(0, NLAT // 128, block, 0)
        return 0

    lax.fori_loop(0, STEPS, step, 0)

    nslot = BANDS * SLOTS
    slot = lax.broadcasted_iota(jnp.int32, (1, nslot), 1)
    south = x_ref[240:241, 0:nslot] + (slot % 256 // 8 * LAT - MARG).astype(F32)
    low = x_ref[242:243, 0:nslot]
    high = x_ref[244:245, 0:nslot]
    for lo in range(LO):
        r = lax.broadcasted_iota(jnp.int32, (256, 1), 0)
        place = (r // 8 * LAT + lo * 8 + r % 8).astype(F32)
        t_ref[lo * 256 : (lo + 1) * 256, :] = jnp.where(
            place == south, low, jnp.where(place == south + 1.0, high, 0.0)
        ).astype(BF)
    flux = jnp.concatenate([f_ref[n].astype(BF) for n in range(NLAT // 128)], axis=1)
    at_slots = jnp.dot(flux, t_ref[...], preferred_element_type=F32) * (-ocean_step / math.sqrt(COLS))
    ends = jnp.concatenate(
        [x_ref[0:128, n * 128 : (n + 1) * 128].T.astype(BF) for n in range(NLAT // 128)], axis=0
    )
    ends = jnp.concatenate([ends[lo * 256 : (lo + 1) * 256] for lo in range(LO)], axis=1)
    ends = jnp.dot(ends, se_ref[...], preferred_element_type=F32)
    for u in range(2):
        pieces = []
        for f in range(FIELDS):
            for s in range(4):
                at = s * 256 + u * 128
                pieces.append(at_slots[f * 24 : f * 24 + 24, at : at + 128])
        for i, v in enumerate(block_transpose(pieces, 8)):
            tile = u * 16 + i
            for f in range(FIELDS):
                o_ref[tile * FIELDS + f, 0:24, :] = v.astype(BF)
    for b in range(BANDS):
        for f in range(FIELDS):
            pair = [ends[8 * b : 8 * b + 8, (q * FIELDS + f) * 128 : (q * FIELDS + f + 1) * 128] for q in range(2)]
            o_ref[b * FIELDS + f, 24:40, :] = jnp.concatenate(pair, axis=0).astype(BF)


def ocean_kernel(
    ids, f_ref, zt_ref, z_ref, c_ref, o0_ref, r_ref, so_ref, co_ref, o_ref, w_ref, p_ref, t_ref, h_ref
):
    lon = o_ref.shape[0]
    start = pl.multiple_of(ids[1] * SLOTS, SLOTS)
    o_ref[...] = o0_ref[...]
    scale = 1.0 / math.sqrt(lon)

    def two_steps(j, _):
        pair = jnp.concatenate([f_ref[2 * j], f_ref[2 * j + 1]], axis=1)
        p_ref[...] = jnp.dot(zt_ref[...], pair, preferred_element_type=F32)
        for i in range(2):
            coarse = o_ref[...].astype(BF)
            pull = jnp.dot(
                jnp.concatenate([coarse, coarse], axis=1), c_ref[...], preferred_element_type=F32
            )
            updated = (o_ref[...] + (pull + p_ref[:, i * 128 : (i + 1) * 128])) * r_ref[...]
            o_ref[...] = updated
            w_ref[:, i * 128 : (i + 1) * 128] = updated.astype(BF)
        coef = jnp.dot(z_ref[...], w_ref[...], preferred_element_type=F32) * scale
        for i in range(2):
            h_ref[i] = coef[:, i * 128 : (i + 1) * 128].T
            at = pl.multiple_of((2 * j + i) * SLOTS, SLOTS)
            t_ref[pl.ds(at, SLOTS), :] = h_ref[i, pl.ds(start, SLOTS), :]
        return 0

    lax.fori_loop(0, STEPS // 2, two_steps, 0)
    co_ref[...] = jnp.dot(t_ref[...].astype(BF), join_columns(), preferred_element_type=F32).astype(BF)
    for x in range(0, lon, 128):
        w = min(128, lon - x)
        h_ref[0, :, 0:w] = o_ref[x : x + w, :].T
        so_ref[:, x : x + w] = h_ref[0, pl.ds(start, SLOTS), 0:w]


def unpack_kernel(b_ref, o_ref, t_ref, v_ref):
    def take(m, _):
        t_ref[pl.ds(pl.multiple_of(m * 16, 16), 16), :] = b_ref[m, 24:40, :].astype(F32)
        return 0

    lax.fori_loop(0, WAVES, take, 0)
    for q in range(2):
        for h in range(8):
            v = t_ref[pl.ds(q * 8 + h, WAVES, stride=16), :].T
            for i in range(4 if q == 0 else 1):
                for c in range(2):
                    at = i * 32 + c * LEVELS
                    v_ref[c, pl.ds((4 * q + i) * 8 + h, LEVELS, stride=LAT), :] = v[at : at + LEVELS]
    both = jnp.concatenate([v_ref[0], v_ref[1]], axis=1).astype(BF)
    o_ref[...] = jnp.dot(both, join_columns(), preferred_element_type=F32)


def vmem(n):
    return [pl.BlockSpec(memory_space=pltpu.VMEM)] * n


def smem(n):
    return [pl.BlockSpec(memory_space=pltpu.SMEM)] * n


def call(kernel, in_specs, out_shape, scratch):
    return pl.pallas_call(
        kernel,
        out_shape=out_shape,
        in_specs=in_specs,
        out_specs=jax.tree.map(lambda _: pl.BlockSpec(memory_space=pltpu.VMEM), out_shape),
        scratch_shapes=scratch,
    )


def shape(dims, kind):
    return jax.ShapeDtypeStruct(dims, kind)


def per_device(
    air_fourier_coefficients,
    quadrature_factor,
    associated_polynomial_table,
    east_west_harmonic,
    boundary_diffusion,
    bulk_transfer_coefficient,
    skin_heat_earlier,
    sea_boundary_values,
    sea_damping_speed,
    sea_coupling_matrix,
    patch_active_entries,
    sea_southern_parallel,
    sea_northern_share,
    air_paired_cells,
    air_second_share,
):
    band = lax.axis_index("band")
    lev = lax.axis_index("lev")
    ids = jnp.stack([band, lev]).astype(jnp.int32)
    lon = sea_boundary_values.shape[2]
    degree_count = associated_polynomial_table.shape[2]

    chunks = call(
        pack_kernel,
        smem(2) + vmem(8),
        shape((WAVES, CHUNK, 128), BF),
        [pltpu.VMEM((2, ITEMS * LAT, 128), F32), pltpu.VMEM((WAVES * XROWS, 128), F32)],
    )(
        ids,
        patch_active_entries,
        air_fourier_coefficients.reshape(LEVELS * LAT, COLS),
        skin_heat_earlier.reshape(STEPS * LAT, COLS),
        boundary_diffusion.reshape(LEVELS * LEVELS, LAT),
        quadrature_factor[None],
        bulk_transfer_coefficient,
        sea_southern_parallel[None],
        sea_northern_share[None],
        jnp.asarray(pair_matrix(), BF),
    )
    got = lax.all_to_all(chunks, AXES, 0, 0, tiled=True)

    operator = call(
        operator_kernel,
        smem(2) + [pl.BlockSpec(memory_space=pl.ANY)],
        shape((NLAT, NLAT), BF),
        [
            pltpu.VMEM((LO, BANDS, 8, degree_count), BF),
            pltpu.VMEM((NLAT, degree_count), BF),
            pltpu.SemaphoreType.DMA((LO,)),
        ],
    )(ids, east_west_harmonic, associated_polynomial_table.reshape(FIELDS, BANDS, LO, 8, degree_count))

    row = jnp.arange(NPAIR * 8, dtype=jnp.int32)[:, None]
    col = jnp.arange(FIELDS * 128, dtype=jnp.int32)[None, :]
    select_mix = ((row // 8 == col % 128) & (row % 8 // 2 == col // 128)).astype(BF)
    row = jnp.arange(ITEMS * 8, dtype=jnp.int32)[:, None]
    item = row // 8
    same = (col % ITEMS == item) & (col // 128 == row % 8 // 2)
    same_c = (col % 64 // ITEMS == row % 2) | (item == 28) | (item == 29)
    select_x = jnp.stack([same & same_c & (col % 128 // 64 == q) for q in range(2)]).astype(BF)
    row = jnp.arange(LO * 128, dtype=jnp.int32)[:, None]
    col = jnp.arange(2 * FIELDS * 128, dtype=jnp.int32)[None, :]
    lo = col // 512 * 4 + col % 128 // 32
    at = lo * 128 + col % LEVELS * 8 + col % 512 // 128 * 2 + col % 32 // LEVELS
    select_end = (row == at).astype(BF)

    part = jnp.arange(160, dtype=jnp.int32)[:, None]
    longitude = jnp.where(part < 80, part % 40, part % 40 * 40)
    phases = longitude * east_west_harmonic[None, :] % lon
    angles = phases.astype(F32) * (2.0 * math.pi / lon)
    angle_parts = jnp.where(part // 40 % 2 == 0, jnp.cos(angles), jnp.sin(angles))
    own_sea, own_damp, operator = lax.optimization_barrier((sea_boundary_values[0], sea_damping_speed[0], operator))
    sent = jnp.concatenate([own_sea.astype(BF), own_damp.astype(BF)], axis=0)
    others = []
    for d in range(1, FIELDS):
        others.append(lax.ppermute(sent, "lev", [(i, (i + d) % FIELDS) for i in range(FIELDS)]))
    zonal_t, zonal, ocean0, shrink, couple = call(
        tables_kernel,
        smem(2) + vmem(6),
        (
            shape((lon, COLS), BF),
            shape((COLS, lon), BF),
            shape((lon, 128), F32),
            shape((lon, 128), F32),
            shape((256, 128), BF),
        ),
        [pltpu.VMEM((lon, COLS), F32), pltpu.VMEM((2, 128, lon), F32)],
    )(ids, sea_coupling_matrix, angle_parts, own_sea, own_damp, *others)

    got, zonal_t, zonal, ocean0, shrink, couple = lax.optimization_barrier(
        (got, zonal_t, zonal, ocean0, shrink, couple)
    )
    got = got.reshape(BANDS, FIELDS, 8, 8, 128).transpose(1, 2, 0, 3, 4).reshape(FIELDS, 8, 256, 128)
    out = call(
        atmosphere_kernel,
        vmem(5),
        shape((WAVES, OUT_ROWS, 128), BF),
        [
            pltpu.VMEM((NPAIR * 8, NLAT), F32),
            pltpu.VMEM((ITEMS * 8, NLAT), F32),
            pltpu.VMEM((128, NLAT), F32),
            pltpu.VMEM((NLAT // 128, STEPS * 8, 128), F32),
            pltpu.VMEM((NLAT, BANDS * SLOTS), BF),
        ],
    )(got, select_mix, select_x, select_end, operator)

    back = lax.all_to_all(out, AXES, 0, 0, tiled=True)
    flux_in = back[:, :24].reshape(WAVES, 2, STEPS, 128).transpose(2, 1, 0, 3).reshape(STEPS, COLS, 128)
    sea_end, ocean_coef = call(
        ocean_kernel,
        smem(1) + vmem(6),
        (shape((SLOTS, lon), F32), shape((STEPS * SLOTS, COLS), BF)),
        [
            pltpu.VMEM((lon, 128), F32),
            pltpu.VMEM((lon, COLS), BF),
            pltpu.VMEM((lon, COLS), F32),
            pltpu.VMEM((STEPS * SLOTS, COLS), F32),
            pltpu.VMEM((2, 128, COLS), F32),
        ],
    )(ids, flux_in, zonal_t, zonal, couple, ocean0, shrink)
    ocean_coef = ocean_coef.reshape(STEPS, SLOTS, COLS)
    air_coefficients_end = call(
        unpack_kernel,
        vmem(1),
        shape((LEVELS * LAT, COLS), F32),
        [pltpu.VMEM((WAVES * 16, 128), F32), pltpu.VMEM((2, LEVELS * LAT, 128), F32)],
    )(back).reshape(1, LEVELS, LAT, COLS)

    up = [(i, i + 1) for i in range(BANDS - 1)]
    down = [(j, i) for i, j in up]
    before = lax.ppermute(ocean_coef, "band", up)
    after = lax.ppermute(ocean_coef, "band", down)
    neighbours = jnp.concatenate([before, ocean_coef, after], axis=1)
    slot_index = jnp.arange(3 * SLOTS, dtype=jnp.int32)[None, :]
    first = (air_paired_cells[0] - (band - 1) * SLOTS)[:, None]
    second = (air_paired_cells[1] - (band - 1) * SLOTS)[:, None]
    return_taps = jnp.where(slot_index == first, (1.0 - air_second_share)[:, None], 0.0) + jnp.where(
        slot_index == second, air_second_share[:, None], 0.0
    )
    skin_heat_newest = jnp.einsum(
        "ga,kac->kgc", return_taps.astype(BF), neighbours, preferred_element_type=F32
    )[:, None]
    return (air_coefficients_end, sea_end[None], skin_heat_newest)


def solution(mesh):
    return jax.shard_map(
        per_device,
        mesh=mesh,
        in_specs=(
            P("lev", None, "band", None),
            P("band"),
            P("band", None, None),
            P(),
            P("lev", None, None, "band"),
            P("lev", "band"),
            P(None, "lev", "band", None),
            P("lev", "band", None),
            P("lev", "band", None),
            P(),
            P("band"),
            P("band"),
            P("band"),
            P(None, "band"),
            P("band"),
        ),
        out_specs=(
            P("lev", None, "band", None),
            P("lev", "band", None),
            P(None, "lev", "band", None),
        ),
        check_vma=False,
    )
```

```python
import math

import jax
import jax.numpy as jnp
import numpy as np
from jax import lax
from jax.experimental import pallas as pl
from jax.experimental.pallas import tpu as pltpu
from jax.sharding import PartitionSpec as P


MARG = 8
AXES = ("band", "lev")
degree_damping = 2e-06
ocean_step = 0.5
mixing_diagonal = 0.95
synth_divisor = 4.0

BANDS, FIELDS = 32, 4
LEVELS, LAT, COLS = 16, 40, 256
NLAT = BANDS * LAT
WAVES = COLS // 2
STEPS = 12
SLOTS = 32
LO = LAT // 8
ITEMS = 32
PAIRS = [(l, p) for l in range(LEVELS) for p in range(l + 1, LEVELS)]
NPAIR = len(PAIRS)
XROWS = 24
OUT_ROWS = 40
CHUNK = XROWS + LAT
BF = jnp.bfloat16
F32 = jnp.float32
NT = (((1,), (1,)), ((), ()))


def pair_matrix():
    q = np.zeros((LEVELS * LEVELS, 128), np.float32)
    for i, (l, p) in enumerate(PAIRS):
        q[l * LEVELS + p, i] = 1.0
        q[p * LEVELS + l, i] = -1.0
    return q


def hi_lo(v):
    hi = v.astype(BF)
    return hi, (v - hi.astype(F32)).astype(BF)


def split_columns():
    row = lax.broadcasted_iota(jnp.int32, (COLS, COLS), 0)
    col = lax.broadcasted_iota(jnp.int32, (COLS, COLS), 1)
    return jnp.where(row == 2 * (col % WAVES) + col // WAVES, 1.0, 0.0).astype(BF)


def join_columns():
    row = lax.broadcasted_iota(jnp.int32, (COLS, COLS), 0)
    col = lax.broadcasted_iota(jnp.int32, (COLS, COLS), 1)
    return jnp.where(col == 2 * (row % WAVES) + row // WAVES, 1.0, 0.0).astype(BF)


def block_transpose(arrays, width):
    arrays = list(arrays)
    block = lax.broadcasted_iota(jnp.int32, arrays[0].shape, 1) // width
    s = 1
    while s < len(arrays):
        upper = (block & s) != 0
        for i in range(len(arrays)):
            if not i & s:
                a, b = arrays[i], arrays[i | s]
                arrays[i] = jnp.where(upper, pltpu.roll(b, s * width, 1), a)
                arrays[i | s] = jnp.where(upper, b, pltpu.roll(a, 128 - s * width, 1))
        s *= 2
    return arrays


def pack_kernel(ids, live_ref, x_ref, s_ref, b_ref, w_ref, k_ref, south_ref, north_ref, q_ref, o_ref, d_ref, t_ref):
    spread = split_columns()
    base = 0
    for ref in (x_ref, s_ref):
        n = ref.shape[0]
        d = jnp.dot(ref[...].astype(BF), spread, preferred_element_type=F32)
        d_ref[0, base : base + n, :] = d[:, :WAVES]
        d_ref[1, base : base + n, :] = d[:, WAVES:]
        base += n
    slot = lax.broadcasted_iota(jnp.int32, (1, SLOTS), 1)
    live = slot < live_ref[0]
    offset = (south_ref[...] - (ids[0] * LAT - MARG)).astype(F32)
    low = jnp.where(live, 1.0 - north_ref[...], 0.0)
    high = jnp.where(live, north_ref[...], 0.0)
    kind = jnp.full((1, SLOTS), ids[1], jnp.int32)
    taps = jnp.where(kind == 0, offset, jnp.where(kind == 1, low, high))
    taps = jnp.concatenate([taps, jnp.zeros((1, LAT - SLOTS), F32)], axis=1)
    w_hi, w_lo = hi_lo(w_ref[...])
    k_hi, k_lo = hi_lo(k_ref[...])
    rows = [w_hi.astype(F32), w_lo.astype(F32), k_hi.astype(F32), k_lo.astype(F32), taps]
    small = jnp.concatenate(rows + [jnp.zeros((3, LAT), F32)], axis=0).T
    for c in range(2):
        for i, pick in enumerate((c, 2 + c, 4)):
            d_ref[c, (28 + i) * LAT : (29 + i) * LAT, :] = jnp.broadcast_to(
                small[:, pick : pick + 1], (LAT, WAVES)
            )
        d_ref[c, 31 * LAT : 32 * LAT, :] = jnp.zeros((LAT, WAVES), F32)
    m_hi, m_lo = hi_lo(b_ref[...].T)
    mix = jnp.dot(m_hi, q_ref[...], preferred_element_type=F32)
    mix = (mix + jnp.dot(m_lo, q_ref[...], preferred_element_type=F32)).astype(BF)
    for j in range(XROWS // 8):
        for h in range(8):
            parts = []
            for q in range(2):
                for c in range(2):
                    lo = 2 * j + q
                    if lo < LO:
                        parts.append(d_ref[c, pl.ds(lo * 8 + h, ITEMS, stride=LAT), :])
                    else:
                        parts.append(jnp.zeros((ITEMS, WAVES), F32))
            t_ref[pl.ds(j * 8 + h, WAVES, stride=XROWS), :] = jnp.concatenate(parts, axis=0).T

    def put(m, _):
        o_ref[m, 0:XROWS, :] = t_ref[pl.ds(pl.multiple_of(m * XROWS, 8), XROWS), :].astype(BF)
        o_ref[m, XROWS:CHUNK, :] = mix
        return 0

    lax.fori_loop(0, WAVES, put, 0)


def operator_kernel(ids, wave_ref, table_ref, p_ref, t_ref, d_ref, sem):
    def copy(lo):
        return pltpu.make_async_copy(table_ref.at[ids[1], :, lo], t_ref.at[lo], sem.at[lo])

    for lo in range(LO):
        copy(lo).start()
    degree_count = p_ref.shape[1]
    wave = wave_ref[ids[0] * FIELDS + ids[1]]
    degrees = wave + lax.broadcasted_iota(jnp.int32, (1, degree_count), 1)
    degree_float = degrees.astype(F32)
    damping = 1.0 / (1.0 + degree_damping * degree_float * (degree_float + 1.0))
    damping = jnp.where(degrees < degree_count, damping, 0.0)
    scale = 1.0 / (synth_divisor * math.sqrt(degree_count) * math.sqrt(NLAT))
    for lo in range(LO):
        copy(lo).wait()
        part = t_ref[lo].reshape(BANDS * 8, degree_count)
        d_ref[lo * 256 : (lo + 1) * 256, :] = (part.astype(F32) * damping).astype(BF)
    for lo in range(LO):
        part = t_ref[lo].reshape(BANDS * 8, degree_count)
        p = lax.dot_general(part, d_ref[...], NT, preferred_element_type=F32)
        p_ref[lo * 256 : (lo + 1) * 256, :] = (p * scale).astype(BF)


def tables_kernel(ids, c_ref, a_ref, own_s, own_d, o1, o2, o3, zt_ref, z_ref, so_ref, sr_ref, cp_ref, w_ref, h_ref):
    lon = own_s.shape[1]
    fine = a_ref[0:80, :]
    for q in range(lon // 40):
        ca = a_ref[80 + q : 81 + q, :]
        sa = a_ref[120 + q : 121 + q, :]
        cos = ca * fine[0:40] - sa * fine[40:80]
        sin = sa * fine[0:40] + ca * fine[40:80]
        w_ref[40 * q : 40 * q + 40, 0:WAVES] = cos
        w_ref[40 * q : 40 * q + 40, WAVES:COLS] = -sin
    zt_ref[...] = w_ref[...].astype(BF)
    for x in range(0, lon, 128):
        w = min(128, lon - x)
        for c in range(2):
            z_ref[c * WAVES : (c + 1) * WAVES, x : x + w] = (
                w_ref[x : x + w, c * WAVES : (c + 1) * WAVES].T.astype(BF)
            )
    for j, (sea, damp) in enumerate(
        [(own_s[...], own_d[...])] + [(o[0:SLOTS, :], o[SLOTS:, :]) for o in (o1, o2, o3)]
    ):
        field = (ids[1] + FIELDS - j) % FIELDS
        at = pl.multiple_of(field * SLOTS, SLOTS)
        h_ref[0, pl.ds(at, SLOTS), :] = sea.astype(F32)
        h_ref[1, pl.ds(at, SLOTS), :] = damp.astype(F32)
    for x in range(0, lon, 128):
        w = min(128, lon - x)
        so_ref[x : x + w, :] = h_ref[0, :, x : x + w].T
        sr_ref[x : x + w, :] = 1.0 / (1.0 + ocean_step * h_ref[1, :, x : x + w].T)
    row = lax.broadcasted_iota(jnp.int32, (128, 128), 0)
    col = lax.broadcasted_iota(jnp.int32, (128, 128), 1)
    same = row % SLOTS == col % SLOTS
    couple = jnp.zeros((128, 128), F32)
    for e in range(FIELDS):
        for f in range(FIELDS):
            v = ocean_step * (c_ref[f, e] - c_ref[e, f])
            couple = jnp.where(same & (row // SLOTS == e) & (col // SLOTS == f), v, couple)
    hi, lo = hi_lo(couple)
    cp_ref[0:128, :] = hi
    cp_ref[128:256, :] = lo


def atmosphere_kernel(
    g_ref, sm_ref, sx_ref, se_ref, p_ref, o_ref, a_ref, x_ref, y_ref, s_ref, f_ref, t_ref
):
    for lo in range(LO):
        lanes = slice(lo * 256, (lo + 1) * 256)
        mix = jnp.concatenate([g_ref[f, 3 + lo] for f in range(FIELDS)], axis=1)
        a_ref[:, lanes] = lax.dot_general(sm_ref[...], mix, NT, preferred_element_type=F32)
        rows = jnp.concatenate([g_ref[f, lo // 2] for f in range(FIELDS)], axis=1)
        x_ref[:, lanes] = lax.dot_general(sx_ref[lo % 2], rows, NT, preferred_element_type=F32)

    weight = x_ref[28 * 8 : 29 * 8, :]
    for l in range(0, LEVELS, 2):
        pair = x_ref[8 * l : 8 * l + 16, :].reshape(2, 8, NLAT) * weight[None]
        s_ref[0, 8 * l : 8 * l + 16, :] = pair.reshape(16, NLAT).astype(BF)

    def mix_block(k, n, half):
        lanes = slice(n * 256 + half * 128, n * 256 + half * 128 + 128)
        mid = [
            x_ref[8 * l : 8 * l + 8, lanes] - y_ref[n, 8 * l : 8 * l + 8, half * 128 : half * 128 + 128]
            for l in range(LEVELS)
        ]
        skin = x_ref[pl.ds(pl.multiple_of(128 + 8 * k, 8), 8), lanes]
        flux = x_ref[29 * 8 : 30 * 8, lanes] * (skin - mid[LEVELS - 1])
        f_ref[2 * n + half, pl.ds(k, 8, stride=STEPS), :] = flux
        acc = [mixing_diagonal * v for v in mid]
        acc[LEVELS - 1] = acc[LEVELS - 1] + flux
        for i, (l, p) in enumerate(PAIRS):
            a = a_ref[8 * i : 8 * i + 8, lanes]
            acc[l] = acc[l] + a * mid[p]
            acc[p] = acc[p] - a * mid[l]
        scale = x_ref[28 * 8 : 29 * 8, lanes]
        for l in range(LEVELS):
            x_ref[8 * l : 8 * l + 8, lanes] = acc[l]
        for l in range(0, LEVELS, 2):
            pair = jnp.concatenate([acc[l] * scale, acc[l + 1] * scale], axis=0)
            s_ref[1 - k % 2, 8 * l : 8 * l + 16, lanes] = pair.astype(BF)

    def step(k, _):
        for n in range(LO + 1):
            if n < LO:
                y_ref[n] = jnp.dot(
                    s_ref[k % 2], p_ref[:, n * 256 : (n + 1) * 256], preferred_element_type=F32
                )
            if n > 0:
                mix_block(k, n - 1, 0)
                mix_block(k, n - 1, 1)
        return 0

    lax.fori_loop(0, STEPS, step, 0)

    nslot = BANDS * SLOTS
    slot = lax.broadcasted_iota(jnp.int32, (1, nslot), 1)
    south = x_ref[240:241, 0:nslot] + (slot % 256 // 8 * LAT - MARG).astype(F32)
    low = x_ref[242:243, 0:nslot]
    high = x_ref[244:245, 0:nslot]
    for lo in range(LO):
        r = lax.broadcasted_iota(jnp.int32, (256, 1), 0)
        place = (r // 8 * LAT + lo * 8 + r % 8).astype(F32)
        t_ref[lo * 256 : (lo + 1) * 256, :] = jnp.where(
            place == south, low, jnp.where(place == south + 1.0, high, 0.0)
        ).astype(BF)
    flux = jnp.concatenate([f_ref[n].astype(BF) for n in range(NLAT // 128)], axis=1)
    at_slots = jnp.dot(flux, t_ref[...], preferred_element_type=F32) * (-ocean_step / math.sqrt(COLS))
    ends = jnp.concatenate(
        [x_ref[0:128, n * 128 : (n + 1) * 128].T.astype(BF) for n in range(NLAT // 128)], axis=0
    )
    ends = jnp.concatenate([ends[lo * 256 : (lo + 1) * 256] for lo in range(LO)], axis=1)
    ends = jnp.dot(ends, se_ref[...], preferred_element_type=F32)
    for u in range(2):
        pieces = []
        for f in range(FIELDS):
            for s in range(4):
                at = s * 256 + u * 128
                pieces.append(at_slots[f * 24 : f * 24 + 24, at : at + 128])
        for i, v in enumerate(block_transpose(pieces, 8)):
            tile = u * 16 + i
            for f in range(FIELDS):
                o_ref[tile * FIELDS + f, 0:24, :] = v.astype(BF)
    for b in range(BANDS):
        for f in range(FIELDS):
            pair = [ends[8 * b : 8 * b + 8, (q * FIELDS + f) * 128 : (q * FIELDS + f + 1) * 128] for q in range(2)]
            o_ref[b * FIELDS + f, 24:40, :] = jnp.concatenate(pair, axis=0).astype(BF)


def ocean_kernel(
    ids, f_ref, zt_ref, z_ref, c_ref, o0_ref, r_ref, so_ref, co_ref, o_ref, w_ref, p_ref, t_ref, h_ref
):
    lon = o_ref.shape[0]
    start = pl.multiple_of(ids[1] * SLOTS, SLOTS)
    o_ref[...] = o0_ref[...]
    scale = 1.0 / math.sqrt(lon)

    def two_steps(j, _):
        pair = jnp.concatenate([f_ref[2 * j], f_ref[2 * j + 1]], axis=1)
        p_ref[...] = jnp.dot(zt_ref[...], pair, preferred_element_type=F32)
        for i in range(2):
            coarse = o_ref[...].astype(BF)
            pull = jnp.dot(
                jnp.concatenate([coarse, coarse], axis=1), c_ref[...], preferred_element_type=F32
            )
            updated = (o_ref[...] + (pull + p_ref[:, i * 128 : (i + 1) * 128])) * r_ref[...]
            o_ref[...] = updated
            w_ref[:, i * 128 : (i + 1) * 128] = updated.astype(BF)
        coef = jnp.dot(z_ref[...], w_ref[...], preferred_element_type=F32) * scale
        for i in range(2):
            h_ref[i] = coef[:, i * 128 : (i + 1) * 128].T
            at = pl.multiple_of((2 * j + i) * SLOTS, SLOTS)
            t_ref[pl.ds(at, SLOTS), :] = h_ref[i, pl.ds(start, SLOTS), :]
        return 0

    lax.fori_loop(0, STEPS // 2, two_steps, 0)
    co_ref[...] = jnp.dot(t_ref[...].astype(BF), join_columns(), preferred_element_type=F32).astype(BF)
    for x in range(0, lon, 128):
        w = min(128, lon - x)
        h_ref[0, :, 0:w] = o_ref[x : x + w, :].T
        so_ref[:, x : x + w] = h_ref[0, pl.ds(start, SLOTS), 0:w]


def unpack_kernel(b_ref, o_ref, t_ref, v_ref):
    def take(m, _):
        t_ref[pl.ds(pl.multiple_of(m * 16, 16), 16), :] = b_ref[m, 24:40, :].astype(F32)
        return 0

    lax.fori_loop(0, WAVES, take, 0)
    for q in range(2):
        for h in range(8):
            v = t_ref[pl.ds(q * 8 + h, WAVES, stride=16), :].T
            for i in range(4 if q == 0 else 1):
                for c in range(2):
                    at = i * 32 + c * LEVELS
                    v_ref[c, pl.ds((4 * q + i) * 8 + h, LEVELS, stride=LAT), :] = v[at : at + LEVELS]
    both = jnp.concatenate([v_ref[0], v_ref[1]], axis=1).astype(BF)
    o_ref[...] = jnp.dot(both, join_columns(), preferred_element_type=F32)


def vmem(n):
    return [pl.BlockSpec(memory_space=pltpu.VMEM)] * n


def smem(n):
    return [pl.BlockSpec(memory_space=pltpu.SMEM)] * n


def call(kernel, in_specs, out_shape, scratch):
    return pl.pallas_call(
        kernel,
        out_shape=out_shape,
        in_specs=in_specs,
        out_specs=jax.tree.map(lambda _: pl.BlockSpec(memory_space=pltpu.VMEM), out_shape),
        scratch_shapes=scratch,
    )


def shape(dims, kind):
    return jax.ShapeDtypeStruct(dims, kind)


def per_device(
    air_fourier_coefficients,
    quadrature_factor,
    associated_polynomial_table,
    east_west_harmonic,
    boundary_diffusion,
    bulk_transfer_coefficient,
    skin_heat_earlier,
    sea_boundary_values,
    sea_damping_speed,
    sea_coupling_matrix,
    patch_active_entries,
    sea_southern_parallel,
    sea_northern_share,
    air_paired_cells,
    air_second_share,
):
    band = lax.axis_index("band")
    lev = lax.axis_index("lev")
    ids = jnp.stack([band, lev]).astype(jnp.int32)
    lon = sea_boundary_values.shape[2]
    degree_count = associated_polynomial_table.shape[2]

    chunks = call(
        pack_kernel,
        smem(2) + vmem(8),
        shape((WAVES, CHUNK, 128), BF),
        [pltpu.VMEM((2, ITEMS * LAT, 128), F32), pltpu.VMEM((WAVES * XROWS, 128), F32)],
    )(
        ids,
        patch_active_entries,
        air_fourier_coefficients.reshape(LEVELS * LAT, COLS),
        skin_heat_earlier.reshape(STEPS * LAT, COLS),
        boundary_diffusion.reshape(LEVELS * LEVELS, LAT),
        quadrature_factor[None],
        bulk_transfer_coefficient,
        sea_southern_parallel[None],
        sea_northern_share[None],
        jnp.asarray(pair_matrix(), BF),
    )
    got = lax.all_to_all(chunks, AXES, 0, 0, tiled=True)

    operator = call(
        operator_kernel,
        smem(2) + [pl.BlockSpec(memory_space=pl.ANY)],
        shape((NLAT, NLAT), BF),
        [
            pltpu.VMEM((LO, BANDS, 8, degree_count), BF),
            pltpu.VMEM((NLAT, degree_count), BF),
            pltpu.SemaphoreType.DMA((LO,)),
        ],
    )(ids, east_west_harmonic, associated_polynomial_table.reshape(FIELDS, BANDS, LO, 8, degree_count))

    row = jnp.arange(NPAIR * 8, dtype=jnp.int32)[:, None]
    col = jnp.arange(FIELDS * 128, dtype=jnp.int32)[None, :]
    select_mix = ((row // 8 == col % 128) & (row % 8 // 2 == col // 128)).astype(BF)
    row = jnp.arange(ITEMS * 8, dtype=jnp.int32)[:, None]
    item = row // 8
    same = (col % ITEMS == item) & (col // 128 == row % 8 // 2)
    same_c = (col % 64 // ITEMS == row % 2) | (item == 28) | (item == 29)
    select_x = jnp.stack([same & same_c & (col % 128 // 64 == q) for q in range(2)]).astype(BF)
    row = jnp.arange(LO * 128, dtype=jnp.int32)[:, None]
    col = jnp.arange(2 * FIELDS * 128, dtype=jnp.int32)[None, :]
    lo = col // 512 * 4 + col % 128 // 32
    at = lo * 128 + col % LEVELS * 8 + col % 512 // 128 * 2 + col % 32 // LEVELS
    select_end = (row == at).astype(BF)

    part = jnp.arange(160, dtype=jnp.int32)[:, None]
    longitude = jnp.where(part < 80, part % 40, part % 40 * 40)
    phases = longitude * east_west_harmonic[None, :] % lon
    angles = phases.astype(F32) * (2.0 * math.pi / lon)
    angle_parts = jnp.where(part // 40 % 2 == 0, jnp.cos(angles), jnp.sin(angles))
    own_sea, own_damp = sea_boundary_values[0], sea_damping_speed[0]
    sent = jnp.concatenate([own_sea.astype(BF), own_damp.astype(BF)], axis=0)
    others = []
    for d in range(1, FIELDS):
        others.append(lax.ppermute(sent, "lev", [(i, (i + d) % FIELDS) for i in range(FIELDS)]))
    zonal_t, zonal, ocean0, shrink, couple = call(
        tables_kernel,
        smem(2) + vmem(6),
        (
            shape((lon, COLS), BF),
            shape((COLS, lon), BF),
            shape((lon, 128), F32),
            shape((lon, 128), F32),
            shape((256, 128), BF),
        ),
        [pltpu.VMEM((lon, COLS), F32), pltpu.VMEM((2, 128, lon), F32)],
    )(ids, sea_coupling_matrix, angle_parts, own_sea, own_damp, *others)

    got = got.reshape(BANDS, FIELDS, 8, 8, 128).transpose(1, 2, 0, 3, 4).reshape(FIELDS, 8, 256, 128)
    out = call(
        atmosphere_kernel,
        vmem(5),
        shape((WAVES, OUT_ROWS, 128), BF),
        [
            pltpu.VMEM((NPAIR * 8, NLAT), F32),
            pltpu.VMEM((ITEMS * 8, NLAT), F32),
            pltpu.VMEM((LO, 128, 256), F32),
            pltpu.VMEM((2, 128, NLAT), BF),
            pltpu.VMEM((NLAT // 128, STEPS * 8, 128), F32),
            pltpu.VMEM((NLAT, BANDS * SLOTS), BF),
        ],
    )(got, select_mix, select_x, select_end, operator)

    back = lax.all_to_all(out, AXES, 0, 0, tiled=True)
    flux_in = back[:, :24].reshape(WAVES, 2, STEPS, 128).transpose(2, 1, 0, 3).reshape(STEPS, COLS, 128)
    sea_end, ocean_coef = call(
        ocean_kernel,
        smem(1) + vmem(6),
        (shape((SLOTS, lon), F32), shape((STEPS * SLOTS, COLS), BF)),
        [
            pltpu.VMEM((lon, 128), F32),
            pltpu.VMEM((lon, COLS), BF),
            pltpu.VMEM((lon, COLS), F32),
            pltpu.VMEM((STEPS * SLOTS, COLS), F32),
            pltpu.VMEM((2, 128, COLS), F32),
        ],
    )(ids, flux_in, zonal_t, zonal, couple, ocean0, shrink)
    ocean_coef = ocean_coef.reshape(STEPS, SLOTS, COLS)
    air_coefficients_end = call(
        unpack_kernel,
        vmem(1),
        shape((LEVELS * LAT, COLS), F32),
        [pltpu.VMEM((WAVES * 16, 128), F32), pltpu.VMEM((2, LEVELS * LAT, 128), F32)],
    )(back).reshape(1, LEVELS, LAT, COLS)

    up = [(i, i + 1) for i in range(BANDS - 1)]
    down = [(j, i) for i, j in up]
    before = lax.ppermute(ocean_coef, "band", up)
    after = lax.ppermute(ocean_coef, "band", down)
    neighbours = jnp.concatenate([before, ocean_coef, after], axis=1)
    slot_index = jnp.arange(3 * SLOTS, dtype=jnp.int32)[None, :]
    first = (air_paired_cells[0] - (band - 1) * SLOTS)[:, None]
    second = (air_paired_cells[1] - (band - 1) * SLOTS)[:, None]
    return_taps = jnp.where(slot_index == first, (1.0 - air_second_share)[:, None], 0.0) + jnp.where(
        slot_index == second, air_second_share[:, None], 0.0
    )
    skin_heat_newest = jnp.einsum(
        "ga,kac->kgc", return_taps.astype(BF), neighbours, preferred_element_type=F32
    )[:, None]
    return (air_coefficients_end, sea_end[None], skin_heat_newest)


def solution(mesh):
    return jax.shard_map(
        per_device,
        mesh=mesh,
        in_specs=(
            P("lev", None, "band", None),
            P("band"),
            P("band", None, None),
            P(),
            P("lev", None, None, "band"),
            P("lev", "band"),
            P(None, "lev", "band", None),
            P("lev", "band", None),
            P("lev", "band", None),
            P(),
            P("band"),
            P("band"),
            P("band"),
            P(None, "band"),
            P("band"),
        ),
        out_specs=(
            P("lev", None, "band", None),
            P("lev", "band", None),
            P(None, "lev", "band", None),
        ),
        check_vma=False,
    )
```

```python
import math

import jax
import jax.numpy as jnp
import numpy as np
from jax import lax
from jax.experimental import pallas as pl
from jax.experimental.pallas import tpu as pltpu
from jax.sharding import PartitionSpec as P


MARG = 8
AXES = ("band", "lev")
degree_damping = 2e-06
ocean_step = 0.5
mixing_diagonal = 0.95
synth_divisor = 4.0

BANDS, FIELDS = 32, 4
LEVELS, LAT, COLS = 16, 40, 256
NLAT = BANDS * LAT
WAVES = COLS // 2
STEPS = 12
SLOTS = 32
LO = LAT // 8
ITEMS = 32
PAIRS = [(l, p) for l in range(LEVELS) for p in range(l + 1, LEVELS)]
NPAIR = len(PAIRS)
XROWS = 24
OUT_ROWS = 40
CHUNK = XROWS + 16
BF = jnp.bfloat16
F32 = jnp.float32
NT = (((1,), (1,)), ((), ()))


def pair_matrix():
    q = np.zeros((LEVELS * LEVELS, 128), np.float32)
    for i, (l, p) in enumerate(PAIRS):
        q[l * LEVELS + p, i] = 1.0
        q[p * LEVELS + l, i] = -1.0
    return q


def hi_lo(v):
    hi = v.astype(BF)
    return hi, (v - hi.astype(F32)).astype(BF)


def split_columns():
    row = lax.broadcasted_iota(jnp.int32, (COLS, COLS), 0)
    col = lax.broadcasted_iota(jnp.int32, (COLS, COLS), 1)
    return jnp.where(row == 2 * (col % WAVES) + col // WAVES, 1.0, 0.0).astype(BF)


def join_columns():
    row = lax.broadcasted_iota(jnp.int32, (COLS, COLS), 0)
    col = lax.broadcasted_iota(jnp.int32, (COLS, COLS), 1)
    return jnp.where(col == 2 * (row % WAVES) + row // WAVES, 1.0, 0.0).astype(BF)


def block_transpose(arrays, width):
    arrays = list(arrays)
    block = lax.broadcasted_iota(jnp.int32, arrays[0].shape, 1) // width
    s = 1
    while s < len(arrays):
        upper = (block & s) != 0
        for i in range(len(arrays)):
            if not i & s:
                a, b = arrays[i], arrays[i | s]
                arrays[i] = jnp.where(upper, pltpu.roll(b, s * width, 1), a)
                arrays[i | s] = jnp.where(upper, b, pltpu.roll(a, 128 - s * width, 1))
        s *= 2
    return arrays


def pack_kernel(ids, live_ref, x_ref, s_ref, b_ref, w_ref, k_ref, south_ref, north_ref, q_ref, o_ref, d_ref, t_ref):
    spread = split_columns()
    base = 0
    for ref in (x_ref, s_ref):
        n = ref.shape[0]
        d = jnp.dot(ref[...].astype(BF), spread, preferred_element_type=F32)
        d_ref[0, base : base + n, :] = d[:, :WAVES]
        d_ref[1, base : base + n, :] = d[:, WAVES:]
        base += n
    slot = lax.broadcasted_iota(jnp.int32, (1, SLOTS), 1)
    live = slot < live_ref[0]
    offset = (south_ref[...] - (ids[0] * LAT - MARG)).astype(F32)
    low = jnp.where(live, 1.0 - north_ref[...], 0.0)
    high = jnp.where(live, north_ref[...], 0.0)
    kind = jnp.full((1, SLOTS), ids[1], jnp.int32)
    taps = jnp.where(kind == 0, offset, jnp.where(kind == 1, low, high))
    taps = jnp.concatenate([taps, jnp.zeros((1, LAT - SLOTS), F32)], axis=1)
    w_hi, w_lo = hi_lo(w_ref[...])
    k_hi, k_lo = hi_lo(k_ref[...])
    rows = [w_hi.astype(F32), w_lo.astype(F32), k_hi.astype(F32), k_lo.astype(F32), taps]
    small = jnp.concatenate(rows + [jnp.zeros((3, LAT), F32)], axis=0).T
    for c in range(2):
        for i, pick in enumerate((c, 2 + c, 4)):
            d_ref[c, (28 + i) * LAT : (29 + i) * LAT, :] = jnp.broadcast_to(
                small[:, pick : pick + 1], (LAT, WAVES)
            )
        d_ref[c, 31 * LAT : 32 * LAT, :] = jnp.zeros((LAT, WAVES), F32)
    m_hi, m_lo = hi_lo(b_ref[...].T)
    mix = jnp.dot(m_hi, q_ref[...], preferred_element_type=F32)
    mix = mix + jnp.dot(m_lo, q_ref[...], preferred_element_type=F32)
    for j in range(XROWS // 8):
        for h in range(8):
            parts = []
            for q in range(2):
                for c in range(2):
                    lo = 2 * j + q
                    if lo < LO:
                        parts.append(d_ref[c, pl.ds(lo * 8 + h, ITEMS, stride=LAT), :])
                    else:
                        parts.append(jnp.zeros((ITEMS, WAVES), F32))
            t_ref[pl.ds(j * 8 + h, WAVES, stride=XROWS), :] = jnp.concatenate(parts, axis=0).T

    upper = lax.broadcasted_iota(jnp.int32, (8, 128), 1) >= 64
    for core in range(2):
        half = mix[32:40] if core else pltpu.roll(mix[32:40], 64, 1)
        spare = jnp.concatenate([jnp.zeros((16, 128), F32), jnp.where(upper, half, 0.0)], axis=0)
        whole = mix[16 * core : 16 * core + 16].astype(BF)

        def put(j, _):
            m = j // FIELDS * (2 * FIELDS) + core * FIELDS + j % FIELDS
            rows = t_ref[pl.ds(pl.multiple_of(m * XROWS, 8), XROWS), :]
            o_ref[m, 0:XROWS, :] = (rows + spare).astype(BF)
            o_ref[m, XROWS:CHUNK, :] = whole
            return 0

        lax.fori_loop(0, WAVES // 2, put, 0)


def operator_kernel(ids, wave_ref, table_ref, p_ref, t_ref, d_ref, sem):
    def copy(lo):
        return pltpu.make_async_copy(table_ref.at[ids[1], :, lo], t_ref.at[lo], sem.at[lo])

    for lo in range(LO):
        copy(lo).start()
    degree_count = p_ref.shape[1]
    wave = wave_ref[ids[0] * FIELDS + ids[1]]
    degrees = wave + lax.broadcasted_iota(jnp.int32, (1, degree_count), 1)
    degree_float = degrees.astype(F32)
    damping = 1.0 / (1.0 + degree_damping * degree_float * (degree_float + 1.0))
    damping = jnp.where(degrees < degree_count, damping, 0.0)
    scale = 1.0 / (synth_divisor * math.sqrt(degree_count) * math.sqrt(NLAT))
    for lo in range(LO):
        copy(lo).wait()
        part = t_ref[lo].reshape(BANDS * 8, degree_count)
        d_ref[lo * 256 : (lo + 1) * 256, :] = (part.astype(F32) * damping).astype(BF)
    for lo in range(LO):
        part = t_ref[lo].reshape(BANDS * 8, degree_count)
        p = lax.dot_general(part, d_ref[...], NT, preferred_element_type=F32)
        p_ref[lo * 256 : (lo + 1) * 256, :] = (p * scale).astype(BF)


def tables_kernel(ids, c_ref, a_ref, own_s, own_d, o1, o2, o3, zt_ref, z_ref, so_ref, sr_ref, cp_ref, w_ref, h_ref):
    lon = own_s.shape[1]
    fine = a_ref[0:80, :]
    for q in range(lon // 40):
        ca = a_ref[80 + q : 81 + q, :]
        sa = a_ref[120 + q : 121 + q, :]
        cos = ca * fine[0:40] - sa * fine[40:80]
        sin = sa * fine[0:40] + ca * fine[40:80]
        w_ref[40 * q : 40 * q + 40, 0:WAVES] = cos
        w_ref[40 * q : 40 * q + 40, WAVES:COLS] = -sin
    zt_ref[...] = w_ref[...].astype(BF)
    for x in range(0, lon, 128):
        w = min(128, lon - x)
        for c in range(2):
            z_ref[c * WAVES : (c + 1) * WAVES, x : x + w] = (
                w_ref[x : x + w, c * WAVES : (c + 1) * WAVES].T.astype(BF)
            )
    for j, (sea, damp) in enumerate(
        [(own_s[...], own_d[...])] + [(o[0:SLOTS, :], o[SLOTS:, :]) for o in (o1, o2, o3)]
    ):
        field = (ids[1] + FIELDS - j) % FIELDS
        at = pl.multiple_of(field * SLOTS, SLOTS)
        h_ref[0, pl.ds(at, SLOTS), :] = sea.astype(F32)
        h_ref[1, pl.ds(at, SLOTS), :] = damp.astype(F32)
    for x in range(0, lon, 128):
        w = min(128, lon - x)
        so_ref[x : x + w, :] = h_ref[0, :, x : x + w].T
        sr_ref[x : x + w, :] = 1.0 / (1.0 + ocean_step * h_ref[1, :, x : x + w].T)
    row = lax.broadcasted_iota(jnp.int32, (128, 128), 0)
    col = lax.broadcasted_iota(jnp.int32, (128, 128), 1)
    same = row % SLOTS == col % SLOTS
    couple = jnp.zeros((128, 128), F32)
    for e in range(FIELDS):
        for f in range(FIELDS):
            v = ocean_step * (c_ref[f, e] - c_ref[e, f])
            couple = jnp.where(same & (row // SLOTS == e) & (col // SLOTS == f), v, couple)
    hi, lo = hi_lo(couple)
    cp_ref[0:128, :] = hi
    cp_ref[128:256, :] = lo


def atmosphere_kernel(
    ids, g_ref, h_ref, sm_ref, sx_ref, se_ref, p_ref, o_ref, a_ref, x_ref, y_ref, s_ref, f_ref, t_ref
):
    first = ids[0] % 2 == 0
    for lo in range(LO):
        lanes = slice(lo * 256, (lo + 1) * 256)
        rows = jnp.concatenate([g_ref[lo // 2, f] for f in range(FIELDS)], axis=1)
        x_ref[:, lanes] = lax.dot_general(sx_ref[lo % 2], rows, NT, preferred_element_type=F32)

    nslot = BANDS * SLOTS
    slot = lax.broadcasted_iota(jnp.int32, (1, nslot), 1)
    south = x_ref[240:241, 0:nslot] + (slot % 256 // 8 * LAT - MARG).astype(F32)
    low = x_ref[242:243, 0:nslot]
    high = x_ref[244:245, 0:nslot]
    for lo in range(LO):
        r = lax.broadcasted_iota(jnp.int32, (256, 1), 0)
        place = (r // 8 * LAT + lo * 8 + r % 8).astype(F32)
        t_ref[lo * 256 : (lo + 1) * 256, :] = jnp.where(
            place == south, low, jnp.where(place == south + 1.0, high, 0.0)
        ).astype(BF)

    for lo in range(LO):
        lanes = slice(lo * 256, (lo + 1) * 256)
        parts = []
        for f in range(FIELDS):
            if lo < 4:
                own, other = g_ref[3 + lo % 2, f], h_ref[1 + lo % 2, f]
                parts.append(jnp.where(first == (lo < 2), own, other))
            else:
                own, other = g_ref[2, f].astype(F32), h_ref[0, f].astype(F32)
                lower = lax.broadcasted_iota(jnp.int32, own.shape, 1) < 64
                even = pltpu.roll(jnp.where(first, own, other), 64, 1)
                parts.append(jnp.where(lower, even, jnp.where(first, other, own)).astype(BF))
        mix = jnp.concatenate(parts, axis=1)
        a_ref[:, lanes] = lax.dot_general(sm_ref[...], mix, NT, preferred_element_type=F32)

    weight = x_ref[28 * 8 : 29 * 8, :]
    for l in range(0, LEVELS, 2):
        pair = x_ref[8 * l : 8 * l + 16, :].reshape(2, 8, NLAT) * weight[None]
        s_ref[0, 8 * l : 8 * l + 16, :] = pair.reshape(16, NLAT).astype(BF)

    def mix_block(k, n, half):
        lanes = slice(n * 256 + half * 128, n * 256 + half * 128 + 128)
        mid = [
            x_ref[8 * l : 8 * l + 8, lanes] - y_ref[n, 8 * l : 8 * l + 8, half * 128 : half * 128 + 128]
            for l in range(LEVELS)
        ]
        skin = x_ref[pl.ds(pl.multiple_of(128 + 8 * k, 8), 8), lanes]
        flux = x_ref[29 * 8 : 30 * 8, lanes] * (skin - mid[LEVELS - 1])
        f_ref[2 * n + half, pl.ds(k, 8, stride=STEPS), :] = flux
        acc = [mixing_diagonal * v for v in mid]
        acc[LEVELS - 1] = acc[LEVELS - 1] + flux
        for i, (l, p) in enumerate(PAIRS):
            a = a_ref[8 * i : 8 * i + 8, lanes]
            acc[l] = acc[l] + a * mid[p]
            acc[p] = acc[p] - a * mid[l]
        scale = x_ref[28 * 8 : 29 * 8, lanes]
        for l in range(LEVELS):
            x_ref[8 * l : 8 * l + 8, lanes] = acc[l]
        for l in range(0, LEVELS, 2):
            pair = jnp.concatenate([acc[l] * scale, acc[l + 1] * scale], axis=0)
            s_ref[1 - k % 2, 8 * l : 8 * l + 16, lanes] = pair.astype(BF)

    def step(k, _):
        for n in range(LO + 1):
            if n < LO:
                y_ref[n] = jnp.dot(
                    s_ref[k % 2], p_ref[:, n * 256 : (n + 1) * 256], preferred_element_type=F32
                )
            if n > 0:
                mix_block(k, n - 1, 0)
                mix_block(k, n - 1, 1)
        return 0

    lax.fori_loop(0, STEPS, step, 0)

    flux = jnp.concatenate([f_ref[n].astype(BF) for n in range(NLAT // 128)], axis=1)
    at_slots = jnp.dot(flux, t_ref[...], preferred_element_type=F32) * (-ocean_step / math.sqrt(COLS))
    ends = jnp.concatenate(
        [x_ref[0:128, n * 128 : (n + 1) * 128].T.astype(BF) for n in range(NLAT // 128)], axis=0
    )
    ends = jnp.concatenate([ends[lo * 256 : (lo + 1) * 256] for lo in range(LO)], axis=1)
    ends = jnp.dot(ends, se_ref[...], preferred_element_type=F32)
    for u in range(2):
        pieces = []
        for f in range(FIELDS):
            for s in range(4):
                at = s * 256 + u * 128
                pieces.append(at_slots[f * 24 : f * 24 + 24, at : at + 128])
        for i, v in enumerate(block_transpose(pieces, 8)):
            tile = u * 16 + i
            for f in range(FIELDS):
                o_ref[tile * FIELDS + f, 0:24, :] = v.astype(BF)
    for b in range(BANDS):
        for f in range(FIELDS):
            pair = [ends[8 * b : 8 * b + 8, (q * FIELDS + f) * 128 : (q * FIELDS + f + 1) * 128] for q in range(2)]
            o_ref[b * FIELDS + f, 24:40, :] = jnp.concatenate(pair, axis=0).astype(BF)


def ocean_kernel(
    ids, f_ref, zt_ref, z_ref, c_ref, o0_ref, r_ref, so_ref, co_ref, o_ref, w_ref, p_ref, t_ref, h_ref
):
    lon = o_ref.shape[0]
    start = pl.multiple_of(ids[1] * SLOTS, SLOTS)
    o_ref[...] = o0_ref[...]
    scale = 1.0 / math.sqrt(lon)

    def two_steps(j, _):
        pair = jnp.concatenate([f_ref[2 * j], f_ref[2 * j + 1]], axis=1)
        p_ref[...] = jnp.dot(zt_ref[...], pair, preferred_element_type=F32)
        for i in range(2):
            coarse = o_ref[...].astype(BF)
            pull = jnp.dot(
                jnp.concatenate([coarse, coarse], axis=1), c_ref[...], preferred_element_type=F32
            )
            updated = (o_ref[...] + (pull + p_ref[:, i * 128 : (i + 1) * 128])) * r_ref[...]
            o_ref[...] = updated
            w_ref[:, i * 128 : (i + 1) * 128] = updated.astype(BF)
        coef = jnp.dot(z_ref[...], w_ref[...], preferred_element_type=F32) * scale
        for i in range(2):
            h_ref[i] = coef[:, i * 128 : (i + 1) * 128].T
            at = pl.multiple_of((2 * j + i) * SLOTS, SLOTS)
            t_ref[pl.ds(at, SLOTS), :] = h_ref[i, pl.ds(start, SLOTS), :]
        return 0

    lax.fori_loop(0, STEPS // 2, two_steps, 0)
    co_ref[...] = jnp.dot(t_ref[...].astype(BF), join_columns(), preferred_element_type=F32).astype(BF)
    for x in range(0, lon, 128):
        w = min(128, lon - x)
        h_ref[0, :, 0:w] = o_ref[x : x + w, :].T
        so_ref[:, x : x + w] = h_ref[0, pl.ds(start, SLOTS), 0:w]


def unpack_kernel(b_ref, o_ref, t_ref, v_ref):
    def take(m, _):
        t_ref[pl.ds(pl.multiple_of(m * 16, 16), 16), :] = b_ref[m, 24:40, :].astype(F32)
        return 0

    lax.fori_loop(0, WAVES, take, 0)
    for q in range(2):
        for h in range(8):
            v = t_ref[pl.ds(q * 8 + h, WAVES, stride=16), :].T
            for i in range(4 if q == 0 else 1):
                for c in range(2):
                    at = i * 32 + c * LEVELS
                    v_ref[c, pl.ds((4 * q + i) * 8 + h, LEVELS, stride=LAT), :] = v[at : at + LEVELS]
    both = jnp.concatenate([v_ref[0], v_ref[1]], axis=1).astype(BF)
    o_ref[...] = jnp.dot(both, join_columns(), preferred_element_type=F32)


def vmem(n):
    return [pl.BlockSpec(memory_space=pltpu.VMEM)] * n


def smem(n):
    return [pl.BlockSpec(memory_space=pltpu.SMEM)] * n


def call(kernel, in_specs, out_shape, scratch):
    return pl.pallas_call(
        kernel,
        out_shape=out_shape,
        in_specs=in_specs,
        out_specs=jax.tree.map(lambda _: pl.BlockSpec(memory_space=pltpu.VMEM), out_shape),
        scratch_shapes=scratch,
    )


def shape(dims, kind):
    return jax.ShapeDtypeStruct(dims, kind)


def per_device(
    air_fourier_coefficients,
    quadrature_factor,
    associated_polynomial_table,
    east_west_harmonic,
    boundary_diffusion,
    bulk_transfer_coefficient,
    skin_heat_earlier,
    sea_boundary_values,
    sea_damping_speed,
    sea_coupling_matrix,
    patch_active_entries,
    sea_southern_parallel,
    sea_northern_share,
    air_paired_cells,
    air_second_share,
):
    band = lax.axis_index("band")
    lev = lax.axis_index("lev")
    ids = jnp.stack([band, lev]).astype(jnp.int32)
    lon = sea_boundary_values.shape[2]
    degree_count = associated_polynomial_table.shape[2]

    chunks = call(
        pack_kernel,
        smem(2) + vmem(8),
        shape((WAVES, CHUNK, 128), BF),
        [pltpu.VMEM((2, ITEMS * LAT, 128), F32), pltpu.VMEM((WAVES * XROWS, 128), F32)],
    )(
        ids,
        patch_active_entries,
        air_fourier_coefficients.reshape(LEVELS * LAT, COLS),
        skin_heat_earlier.reshape(STEPS * LAT, COLS),
        boundary_diffusion.reshape(LEVELS * LEVELS, LAT),
        quadrature_factor[None],
        bulk_transfer_coefficient,
        sea_southern_parallel[None],
        sea_northern_share[None],
        jnp.asarray(pair_matrix(), BF),
    )
    got = lax.all_to_all(chunks, AXES, 0, 0, tiled=True)

    operator = call(
        operator_kernel,
        smem(2) + [pl.BlockSpec(memory_space=pl.ANY)],
        shape((NLAT, NLAT), BF),
        [
            pltpu.VMEM((LO, BANDS, 8, degree_count), BF),
            pltpu.VMEM((NLAT, degree_count), BF),
            pltpu.SemaphoreType.DMA((LO,)),
        ],
    )(ids, east_west_harmonic, associated_polynomial_table.reshape(FIELDS, BANDS, LO, 8, degree_count))

    row = jnp.arange(NPAIR * 8, dtype=jnp.int32)[:, None]
    col = jnp.arange(FIELDS * 128, dtype=jnp.int32)[None, :]
    select_mix = ((row // 8 == col % 128) & (row % 8 // 2 == col // 128)).astype(BF)
    row = jnp.arange(ITEMS * 8, dtype=jnp.int32)[:, None]
    item = row // 8
    same = (col % ITEMS == item) & (col // 128 == row % 8 // 2)
    same_c = (col % 64 // ITEMS == row % 2) | (item == 28) | (item == 29)
    select_x = jnp.stack([same & same_c & (col % 128 // 64 == q) for q in range(2)]).astype(BF)
    row = jnp.arange(LO * 128, dtype=jnp.int32)[:, None]
    col = jnp.arange(2 * FIELDS * 128, dtype=jnp.int32)[None, :]
    lo = col // 512 * 4 + col % 128 // 32
    at = lo * 128 + col % LEVELS * 8 + col % 512 // 128 * 2 + col % 32 // LEVELS
    select_end = (row == at).astype(BF)

    part = jnp.arange(160, dtype=jnp.int32)[:, None]
    longitude = jnp.where(part < 80, part % 40, part % 40 * 40)
    phases = longitude * east_west_harmonic[None, :] % lon
    angles = phases.astype(F32) * (2.0 * math.pi / lon)
    angle_parts = jnp.where(part // 40 % 2 == 0, jnp.cos(angles), jnp.sin(angles))
    own_sea, own_damp = sea_boundary_values[0], sea_damping_speed[0]
    sent = jnp.concatenate([own_sea.astype(BF), own_damp.astype(BF)], axis=0)
    others = []
    for d in range(1, FIELDS):
        others.append(lax.ppermute(sent, "lev", [(i, (i + d) % FIELDS) for i in range(FIELDS)]))
    zonal_t, zonal, ocean0, shrink, couple = call(
        tables_kernel,
        smem(2) + vmem(6),
        (
            shape((lon, COLS), BF),
            shape((COLS, lon), BF),
            shape((lon, 128), F32),
            shape((lon, 128), F32),
            shape((256, 128), BF),
        ),
        [pltpu.VMEM((lon, COLS), F32), pltpu.VMEM((2, 128, lon), F32)],
    )(ids, sea_coupling_matrix, angle_parts, own_sea, own_damp, *others)

    got = got.reshape(BANDS, FIELDS, 5, 8, 128).transpose(2, 1, 0, 3, 4).reshape(5, FIELDS, 256, 128)
    partner = lax.ppermute(got[2:], "band", [(i, i ^ 1) for i in range(BANDS)])
    out = call(
        atmosphere_kernel,
        smem(1) + vmem(6),
        shape((WAVES, OUT_ROWS, 128), BF),
        [
            pltpu.VMEM((NPAIR * 8, NLAT), F32),
            pltpu.VMEM((ITEMS * 8, NLAT), F32),
            pltpu.VMEM((LO, 128, 256), F32),
            pltpu.VMEM((2, 128, NLAT), BF),
            pltpu.VMEM((NLAT // 128, STEPS * 8, 128), F32),
            pltpu.VMEM((NLAT, BANDS * SLOTS), BF),
        ],
    )(ids, got, partner, select_mix, select_x, select_end, operator)

    back = lax.all_to_all(out, AXES, 0, 0, tiled=True)
    flux_in = back[:, :24].reshape(WAVES, 2, STEPS, 128).transpose(2, 1, 0, 3).reshape(STEPS, COLS, 128)
    sea_end, ocean_coef = call(
        ocean_kernel,
        smem(1) + vmem(6),
        (shape((SLOTS, lon), F32), shape((STEPS * SLOTS, COLS), BF)),
        [
            pltpu.VMEM((lon, 128), F32),
            pltpu.VMEM((lon, COLS), BF),
            pltpu.VMEM((lon, COLS), F32),
            pltpu.VMEM((STEPS * SLOTS, COLS), F32),
            pltpu.VMEM((2, 128, COLS), F32),
        ],
    )(ids, flux_in, zonal_t, zonal, couple, ocean0, shrink)
    ocean_coef = ocean_coef.reshape(STEPS, SLOTS, COLS)
    air_coefficients_end = call(
        unpack_kernel,
        vmem(1),
        shape((LEVELS * LAT, COLS), F32),
        [pltpu.VMEM((WAVES * 16, 128), F32), pltpu.VMEM((2, LEVELS * LAT, 128), F32)],
    )(back).reshape(1, LEVELS, LAT, COLS)

    up = [(i, i + 1) for i in range(BANDS - 1)]
    down = [(j, i) for i, j in up]
    before = lax.ppermute(ocean_coef, "band", up)
    after = lax.ppermute(ocean_coef, "band", down)
    neighbours = jnp.concatenate([before, ocean_coef, after], axis=1)
    slot_index = jnp.arange(3 * SLOTS, dtype=jnp.int32)[None, :]
    first = (air_paired_cells[0] - (band - 1) * SLOTS)[:, None]
    second = (air_paired_cells[1] - (band - 1) * SLOTS)[:, None]
    return_taps = jnp.where(slot_index == first, (1.0 - air_second_share)[:, None], 0.0) + jnp.where(
        slot_index == second, air_second_share[:, None], 0.0
    )
    skin_heat_newest = jnp.einsum(
        "ga,kac->kgc", return_taps.astype(BF), neighbours, preferred_element_type=F32
    )[:, None]
    return (air_coefficients_end, sea_end[None], skin_heat_newest)


def solution(mesh):
    return jax.shard_map(
        per_device,
        mesh=mesh,
        in_specs=(
            P("lev", None, "band", None),
            P("band"),
            P("band", None, None),
            P(),
            P("lev", None, None, "band"),
            P("lev", "band"),
            P(None, "lev", "band", None),
            P("lev", "band", None),
            P("lev", "band", None),
            P(),
            P("band"),
            P("band"),
            P("band"),
            P(None, "band"),
            P("band"),
        ),
        out_specs=(
            P("lev", None, "band", None),
            P("lev", "band", None),
            P(None, "lev", "band", None),
        ),
        check_vma=False,
    )
```

```python
import math

import jax
import jax.numpy as jnp
import numpy as np
from jax import lax
from jax.experimental import pallas as pl
from jax.experimental.pallas import tpu as pltpu
from jax.sharding import PartitionSpec as P


MARG = 8
AXES = ("band", "lev")
degree_damping = 2e-06
ocean_step = 0.5
mixing_diagonal = 0.95
synth_divisor = 4.0

BANDS, FIELDS = 32, 4
LEVELS, LAT, COLS = 16, 40, 256
NLAT = BANDS * LAT
WAVES = COLS // 2
STEPS = 12
SLOTS = 32
LO = LAT // 8
ITEMS = 32
PAIRS = [(l, p) for l in range(LEVELS) for p in range(l + 1, LEVELS)]
NPAIR = len(PAIRS)
XROWS = 24
OUT_ROWS = 40
CHUNK = XROWS + 16
BF = jnp.bfloat16
F32 = jnp.float32
NT = (((1,), (1,)), ((), ()))


def pair_matrix():
    q = np.zeros((LEVELS * LEVELS, 128), np.float32)
    for i, (l, p) in enumerate(PAIRS):
        q[l * LEVELS + p, i] = 1.0
        q[p * LEVELS + l, i] = -1.0
    return q


def hi_lo(v):
    hi = v.astype(BF)
    return hi, (v - hi.astype(F32)).astype(BF)


def position():
    return lax.axis_index("band"), lax.axis_index("lev")


def split_columns():
    row = lax.broadcasted_iota(jnp.int32, (COLS, COLS), 0)
    col = lax.broadcasted_iota(jnp.int32, (COLS, COLS), 1)
    return jnp.where(row == 2 * (col % WAVES) + col // WAVES, 1.0, 0.0).astype(BF)


def join_columns():
    row = lax.broadcasted_iota(jnp.int32, (COLS, COLS), 0)
    col = lax.broadcasted_iota(jnp.int32, (COLS, COLS), 1)
    return jnp.where(col == 2 * (row % WAVES) + row // WAVES, 1.0, 0.0).astype(BF)


def block_transpose(arrays, width):
    arrays = list(arrays)
    block = lax.broadcasted_iota(jnp.int32, arrays[0].shape, 1) // width
    s = 1
    while s < len(arrays):
        upper = (block & s) != 0
        for i in range(len(arrays)):
            if not i & s:
                a, b = arrays[i], arrays[i | s]
                arrays[i] = jnp.where(upper, pltpu.roll(b, s * width, 1), a)
                arrays[i | s] = jnp.where(upper, b, pltpu.roll(a, 128 - s * width, 1))
        s *= 2
    return arrays


def pack_kernel(live_ref, x_ref, s_ref, b_ref, w_ref, k_ref, south_ref, north_ref, q_ref, o_ref, d_ref, t_ref):
    ids = position()
    spread = split_columns()
    base = 0
    for ref in (x_ref, s_ref):
        n = ref.shape[0]
        d = jnp.dot(ref[...].astype(BF), spread, preferred_element_type=F32)
        d_ref[0, base : base + n, :] = d[:, :WAVES]
        d_ref[1, base : base + n, :] = d[:, WAVES:]
        base += n
    slot = lax.broadcasted_iota(jnp.int32, (1, SLOTS), 1)
    live = slot < live_ref[0]
    offset = (south_ref[...] - (ids[0] * LAT - MARG)).astype(F32)
    low = jnp.where(live, 1.0 - north_ref[...], 0.0)
    high = jnp.where(live, north_ref[...], 0.0)
    kind = jnp.full((1, SLOTS), ids[1], jnp.int32)
    taps = jnp.where(kind == 0, offset, jnp.where(kind == 1, low, high))
    taps = jnp.concatenate([taps, jnp.zeros((1, LAT - SLOTS), F32)], axis=1)
    w_hi, w_lo = hi_lo(w_ref[...])
    k_hi, k_lo = hi_lo(k_ref[...])
    rows = [w_hi.astype(F32), w_lo.astype(F32), k_hi.astype(F32), k_lo.astype(F32), taps]
    small = jnp.concatenate(rows + [jnp.zeros((3, LAT), F32)], axis=0).T
    for c in range(2):
        for i, pick in enumerate((c, 2 + c, 4)):
            d_ref[c, (28 + i) * LAT : (29 + i) * LAT, :] = jnp.broadcast_to(
                small[:, pick : pick + 1], (LAT, WAVES)
            )
        d_ref[c, 31 * LAT : 32 * LAT, :] = jnp.zeros((LAT, WAVES), F32)
    m_hi, m_lo = hi_lo(b_ref[...].T)
    mix = jnp.dot(m_hi, q_ref[...], preferred_element_type=F32)
    mix = mix + jnp.dot(m_lo, q_ref[...], preferred_element_type=F32)
    for j in range(XROWS // 8):
        for h in range(8):
            parts = []
            for q in range(2):
                for c in range(2):
                    lo = 2 * j + q
                    if lo < LO:
                        parts.append(d_ref[c, pl.ds(lo * 8 + h, ITEMS, stride=LAT), :])
                    else:
                        parts.append(jnp.zeros((ITEMS, WAVES), F32))
            t_ref[pl.ds(j * 8 + h, WAVES, stride=XROWS), :] = jnp.concatenate(parts, axis=0).T

    upper = lax.broadcasted_iota(jnp.int32, (8, 128), 1) >= 64
    for core in range(2):
        half = mix[32:40] if core else pltpu.roll(mix[32:40], 64, 1)
        spare = jnp.concatenate([jnp.zeros((16, 128), F32), jnp.where(upper, half, 0.0)], axis=0)
        whole = mix[16 * core : 16 * core + 16].astype(BF)

        def put(j, _):
            m = j // FIELDS * (2 * FIELDS) + core * FIELDS + j % FIELDS
            rows = t_ref[pl.ds(pl.multiple_of(m * XROWS, 8), XROWS), :]
            o_ref[m, 0:XROWS, :] = (rows + spare).astype(BF)
            o_ref[m, XROWS:CHUNK, :] = whole
            return 0

        lax.fori_loop(0, WAVES // 2, put, 0, unroll=8)


def operator_kernel(wave_ref, table_ref, p_ref, t_ref, d_ref, sem):
    ids = position()

    def copy(lo):
        return pltpu.make_async_copy(table_ref.at[ids[1], :, lo], t_ref.at[lo], sem.at[lo])

    for lo in range(LO):
        copy(lo).start()
    degree_count = p_ref.shape[1]
    wave = wave_ref[ids[0] * FIELDS + ids[1]]
    degrees = wave + lax.broadcasted_iota(jnp.int32, (1, degree_count), 1)
    degree_float = degrees.astype(F32)
    damping = 1.0 / (1.0 + degree_damping * degree_float * (degree_float + 1.0))
    damping = jnp.where(degrees < degree_count, damping, 0.0)
    scale = 1.0 / (synth_divisor * math.sqrt(degree_count) * math.sqrt(NLAT))
    for lo in range(LO):
        copy(lo).wait()
        part = t_ref[lo].reshape(BANDS * 8, degree_count)
        d_ref[lo * 256 : (lo + 1) * 256, :] = (part.astype(F32) * damping).astype(BF)
    for lo in range(LO):
        part = t_ref[lo].reshape(BANDS * 8, degree_count)
        p = lax.dot_general(part, d_ref[...], NT, preferred_element_type=F32)
        p_ref[lo * 256 : (lo + 1) * 256, :] = (p * scale).astype(BF)


def tables_kernel(c_ref, a_ref, own_s, own_d, o1, o2, o3, zt_ref, z_ref, so_ref, sr_ref, cp_ref, w_ref, h_ref):
    ids = position()
    lon = own_s.shape[1]
    fine = a_ref[0:80, :]
    for q in range(lon // 40):
        ca = a_ref[80 + q : 81 + q, :]
        sa = a_ref[120 + q : 121 + q, :]
        cos = ca * fine[0:40] - sa * fine[40:80]
        sin = sa * fine[0:40] + ca * fine[40:80]
        w_ref[40 * q : 40 * q + 40, 0:WAVES] = cos
        w_ref[40 * q : 40 * q + 40, WAVES:COLS] = -sin
    zt_ref[...] = w_ref[...].astype(BF)
    for x in range(0, lon, 128):
        w = min(128, lon - x)
        for c in range(2):
            z_ref[c * WAVES : (c + 1) * WAVES, x : x + w] = (
                w_ref[x : x + w, c * WAVES : (c + 1) * WAVES].T.astype(BF)
            )
    for j, (sea, damp) in enumerate(
        [(own_s[...], own_d[...])] + [(o[0:SLOTS, :], o[SLOTS:, :]) for o in (o1, o2, o3)]
    ):
        field = (ids[1] + FIELDS - j) % FIELDS
        at = pl.multiple_of(field * SLOTS, SLOTS)
        h_ref[0, pl.ds(at, SLOTS), :] = sea.astype(F32)
        h_ref[1, pl.ds(at, SLOTS), :] = damp.astype(F32)
    for x in range(0, lon, 128):
        w = min(128, lon - x)
        so_ref[x : x + w, :] = h_ref[0, :, x : x + w].T
        sr_ref[x : x + w, :] = 1.0 / (1.0 + ocean_step * h_ref[1, :, x : x + w].T)
    row = lax.broadcasted_iota(jnp.int32, (128, 128), 0)
    col = lax.broadcasted_iota(jnp.int32, (128, 128), 1)
    same = row % SLOTS == col % SLOTS
    couple = jnp.zeros((128, 128), F32)
    for e in range(FIELDS):
        for f in range(FIELDS):
            v = ocean_step * (c_ref[f, e] - c_ref[e, f])
            couple = jnp.where(same & (row // SLOTS == e) & (col // SLOTS == f), v, couple)
    hi, lo = hi_lo(couple)
    cp_ref[0:128, :] = hi
    cp_ref[128:256, :] = lo


def atmosphere_kernel(
    g_ref, h_ref, sx_ref, se_ref, p_ref, o_ref, a_ref, x_ref, y_ref, s_ref, f_ref, t_ref
):
    first = position()[0] % 2 == 0
    eye = (
        lax.broadcasted_iota(jnp.int32, (128, 128), 0) == lax.broadcasted_iota(jnp.int32, (128, 128), 1)
    ).astype(F32).astype(BF)
    for lo in range(LO):
        lanes = slice(lo * 256, (lo + 1) * 256)
        rows = jnp.concatenate([g_ref[lo // 2, f] for f in range(FIELDS)], axis=1)
        x_ref[:, lanes] = lax.dot_general(sx_ref[lo % 2], rows, NT, preferred_element_type=F32)

    nslot = BANDS * SLOTS
    slot = lax.broadcasted_iota(jnp.int32, (1, nslot), 1)
    south = x_ref[240:241, 0:nslot] + (slot % 256 // 8 * LAT - MARG).astype(F32)
    low = x_ref[242:243, 0:nslot]
    high = x_ref[244:245, 0:nslot]
    for lo in range(LO):
        r = lax.broadcasted_iota(jnp.int32, (256, 1), 0)
        place = (r // 8 * LAT + lo * 8 + r % 8).astype(F32)
        for col in range(0, nslot, 128):
            at, zero = (0, 144) if col % 256 == 0 else (112, 0)
            lanes = slice(col, col + 128)
            part = place[at : at + 144]
            t_ref[lo * 256 + at : lo * 256 + at + 144, lanes] = jnp.where(
                part == south[:, lanes],
                low[:, lanes],
                jnp.where(part == south[:, lanes] + 1.0, high[:, lanes], 0.0),
            ).astype(BF)
            t_ref[lo * 256 + zero : lo * 256 + zero + 112, lanes] = jnp.zeros((112, 128), BF)

    for lo in range(LO):
        for f in range(FIELDS):
            if lo < 4:
                own, other = g_ref[3 + lo % 2, f], h_ref[1 + lo % 2, f]
                mix = jnp.where(first == (lo < 2), own, other)
            else:
                own, other = g_ref[2, f].astype(F32), h_ref[0, f].astype(F32)
                lower = lax.broadcasted_iota(jnp.int32, own.shape, 1) < 64
                even = pltpu.roll(jnp.where(first, own, other), 64, 1)
                mix = jnp.where(lower, even, jnp.where(first, other, own)).astype(BF)
            turned = lax.dot_general(eye, mix, NT, preferred_element_type=F32)
            for half in range(2):
                for c in range(2):
                    a_ref[2 * lo + half, pl.ds(2 * f + c, NPAIR, stride=8), :] = turned[
                        0:NPAIR, half * 128 : half * 128 + 128
                    ]

    weight = x_ref[28 * 8 : 29 * 8, :]
    for l in range(0, LEVELS, 2):
        pair = x_ref[8 * l : 8 * l + 16, :].reshape(2, 8, NLAT) * weight[None]
        s_ref[0, 8 * l : 8 * l + 16, :] = pair.reshape(16, NLAT).astype(BF)

    def mix_block(k, n, half):
        lanes = slice(n * 256 + half * 128, n * 256 + half * 128 + 128)
        mid = [
            x_ref[8 * l : 8 * l + 8, lanes] - y_ref[n, 8 * l : 8 * l + 8, half * 128 : half * 128 + 128]
            for l in range(LEVELS)
        ]
        skin = x_ref[pl.ds(pl.multiple_of(128 + 8 * k, 8), 8), lanes]
        flux = x_ref[29 * 8 : 30 * 8, lanes] * (skin - mid[LEVELS - 1])
        f_ref[2 * n + half, pl.ds(k, 8, stride=STEPS), :] = flux
        acc = [mixing_diagonal * v for v in mid]
        acc[LEVELS - 1] = acc[LEVELS - 1] + flux
        for i, (l, p) in enumerate(PAIRS):
            a = a_ref[2 * n + half, 8 * i : 8 * i + 8, :]
            acc[l] = acc[l] + a * mid[p]
            acc[p] = acc[p] - a * mid[l]
        scale = x_ref[28 * 8 : 29 * 8, lanes]
        for l in range(LEVELS):
            x_ref[8 * l : 8 * l + 8, lanes] = acc[l]
        for l in range(0, LEVELS, 2):
            pair = jnp.concatenate([acc[l] * scale, acc[l + 1] * scale], axis=0)
            s_ref[1 - k % 2, 8 * l : 8 * l + 16, lanes] = pair.astype(BF)

    def step(k, _):
        for n in range(LO + 1):
            if n < LO:
                y_ref[n] = jnp.dot(
                    s_ref[k % 2], p_ref[:, n * 256 : (n + 1) * 256], preferred_element_type=F32
                )
            if n > 0:
                mix_block(k, n - 1, 0)
                mix_block(k, n - 1, 1)
        return 0

    lax.fori_loop(0, STEPS, step, 0)

    flux = jnp.concatenate([f_ref[n].astype(BF) for n in range(NLAT // 128)], axis=1)
    at_slots = jnp.dot(flux, t_ref[...], preferred_element_type=F32) * (-ocean_step / math.sqrt(COLS))
    ends = jnp.concatenate(
        [x_ref[0:128, n * 128 : (n + 1) * 128].T.astype(BF) for n in range(NLAT // 128)], axis=0
    )
    ends = jnp.concatenate([ends[lo * 256 : (lo + 1) * 256] for lo in range(LO)], axis=1)
    ends = jnp.dot(ends, se_ref[...], preferred_element_type=F32)
    for u in range(2):
        pieces = []
        for f in range(FIELDS):
            for s in range(4):
                at = s * 256 + u * 128
                pieces.append(at_slots[f * 24 : f * 24 + 24, at : at + 128])
        for i, v in enumerate(block_transpose(pieces, 8)):
            tile = u * 16 + i
            for f in range(FIELDS):
                o_ref[tile * FIELDS + f, 0:24, :] = v.astype(BF)
    for b in range(BANDS):
        for f in range(FIELDS):
            pair = [ends[8 * b : 8 * b + 8, (q * FIELDS + f) * 128 : (q * FIELDS + f + 1) * 128] for q in range(2)]
            o_ref[b * FIELDS + f, 24:40, :] = jnp.concatenate(pair, axis=0).astype(BF)


def ocean_kernel(
    f_ref, zt_ref, z_ref, c_ref, o0_ref, r_ref, so_ref, co_ref, o_ref, w_ref, p_ref, t_ref, h_ref
):
    lon = o_ref.shape[0]
    start = pl.multiple_of(position()[1] * SLOTS, SLOTS)
    o_ref[...] = o0_ref[...]
    scale = 1.0 / math.sqrt(lon)

    def two_steps(j, _):
        pair = jnp.concatenate([f_ref[2 * j], f_ref[2 * j + 1]], axis=1)
        p_ref[...] = jnp.dot(zt_ref[...], pair, preferred_element_type=F32)
        for i in range(2):
            coarse = o_ref[...].astype(BF)
            pull = jnp.dot(
                jnp.concatenate([coarse, coarse], axis=1), c_ref[...], preferred_element_type=F32
            )
            updated = (o_ref[...] + (pull + p_ref[:, i * 128 : (i + 1) * 128])) * r_ref[...]
            o_ref[...] = updated
            w_ref[:, i * 128 : (i + 1) * 128] = updated.astype(BF)
        coef = jnp.dot(z_ref[...], w_ref[...], preferred_element_type=F32) * scale
        for i in range(2):
            h_ref[i] = coef[:, i * 128 : (i + 1) * 128].T
            at = pl.multiple_of((2 * j + i) * SLOTS, SLOTS)
            t_ref[pl.ds(at, SLOTS), :] = h_ref[i, pl.ds(start, SLOTS), :]
        return 0

    lax.fori_loop(0, STEPS // 2, two_steps, 0)
    co_ref[...] = jnp.dot(t_ref[...].astype(BF), join_columns(), preferred_element_type=F32).astype(BF)
    for x in range(0, lon, 128):
        w = min(128, lon - x)
        h_ref[0, :, 0:w] = o_ref[x : x + w, :].T
        so_ref[:, x : x + w] = h_ref[0, pl.ds(start, SLOTS), 0:w]


def unpack_kernel(b_ref, o_ref, t_ref, v_ref):
    def take(m, _):
        t_ref[pl.ds(pl.multiple_of(m * 16, 16), 16), :] = b_ref[m, 24:40, :].astype(F32)
        return 0

    lax.fori_loop(0, WAVES, take, 0, unroll=8)
    for q in range(2):
        for h in range(8):
            v = t_ref[pl.ds(q * 8 + h, WAVES, stride=16), :].T
            for i in range(4 if q == 0 else 1):
                for c in range(2):
                    at = i * 32 + c * LEVELS
                    v_ref[c, pl.ds((4 * q + i) * 8 + h, LEVELS, stride=LAT), :] = v[at : at + LEVELS]
    both = jnp.concatenate([v_ref[0], v_ref[1]], axis=1).astype(BF)
    o_ref[...] = jnp.dot(both, join_columns(), preferred_element_type=F32)


def vmem(n):
    return [pl.BlockSpec(memory_space=pltpu.VMEM)] * n


def smem(n):
    return [pl.BlockSpec(memory_space=pltpu.SMEM)] * n


def call(kernel, in_specs, out_shape, scratch):
    return pl.pallas_call(
        kernel,
        out_shape=out_shape,
        in_specs=in_specs,
        out_specs=jax.tree.map(lambda _: pl.BlockSpec(memory_space=pltpu.VMEM), out_shape),
        scratch_shapes=scratch,
    )


def shape(dims, kind):
    return jax.ShapeDtypeStruct(dims, kind)


def per_device(
    air_fourier_coefficients,
    quadrature_factor,
    associated_polynomial_table,
    east_west_harmonic,
    boundary_diffusion,
    bulk_transfer_coefficient,
    skin_heat_earlier,
    sea_boundary_values,
    sea_damping_speed,
    sea_coupling_matrix,
    patch_active_entries,
    sea_southern_parallel,
    sea_northern_share,
    air_paired_cells,
    air_second_share,
):
    band = lax.axis_index("band")
    lon = sea_boundary_values.shape[2]
    degree_count = associated_polynomial_table.shape[2]

    chunks = call(
        pack_kernel,
        smem(1) + vmem(8),
        shape((WAVES, CHUNK, 128), BF),
        [pltpu.VMEM((2, ITEMS * LAT, 128), F32), pltpu.VMEM((WAVES * XROWS, 128), F32)],
    )(
        patch_active_entries,
        air_fourier_coefficients.reshape(LEVELS * LAT, COLS),
        skin_heat_earlier.reshape(STEPS * LAT, COLS),
        boundary_diffusion.reshape(LEVELS * LEVELS, LAT),
        quadrature_factor[None],
        bulk_transfer_coefficient,
        sea_southern_parallel[None],
        sea_northern_share[None],
        jnp.asarray(pair_matrix(), BF),
    )
    got = lax.all_to_all(chunks, AXES, 0, 0, tiled=True)

    operator = call(
        operator_kernel,
        smem(1) + [pl.BlockSpec(memory_space=pl.ANY)],
        shape((NLAT, NLAT), BF),
        [
            pltpu.VMEM((LO, BANDS, 8, degree_count), BF),
            pltpu.VMEM((NLAT, degree_count), BF),
            pltpu.SemaphoreType.DMA((LO,)),
        ],
    )(east_west_harmonic, associated_polynomial_table.reshape(FIELDS, BANDS, LO, 8, degree_count))

    col = jnp.arange(FIELDS * 128, dtype=jnp.int32)[None, :]
    row = jnp.arange(ITEMS * 8, dtype=jnp.int32)[:, None]
    item = row // 8
    same = (col % ITEMS == item) & (col // 128 == row % 8 // 2)
    same_c = (col % 64 // ITEMS == row % 2) | (item == 28) | (item == 29)
    select_x = jnp.stack([same & same_c & (col % 128 // 64 == q) for q in range(2)]).astype(BF)
    row = jnp.arange(LO * 128, dtype=jnp.int32)[:, None]
    col = jnp.arange(2 * FIELDS * 128, dtype=jnp.int32)[None, :]
    lo = col // 512 * 4 + col % 128 // 32
    at = lo * 128 + col % LEVELS * 8 + col % 512 // 128 * 2 + col % 32 // LEVELS
    select_end = (row == at).astype(BF)

    part = jnp.arange(160, dtype=jnp.int32)[:, None]
    longitude = jnp.where(part < 80, part % 40, part % 40 * 40)
    phases = longitude * east_west_harmonic[None, :] % lon
    angles = phases.astype(F32) * (2.0 * math.pi / lon)
    angle_parts = jnp.where(part // 40 % 2 == 0, jnp.cos(angles), jnp.sin(angles))
    own_sea, own_damp = sea_boundary_values[0], sea_damping_speed[0]
    sent = jnp.concatenate([own_sea.astype(BF), own_damp.astype(BF)], axis=0)
    others = []
    for d in range(1, FIELDS):
        others.append(lax.ppermute(sent, "lev", [(i, (i + d) % FIELDS) for i in range(FIELDS)]))
    zonal_t, zonal, ocean0, shrink, couple = call(
        tables_kernel,
        smem(1) + vmem(6),
        (
            shape((lon, COLS), BF),
            shape((COLS, lon), BF),
            shape((lon, 128), F32),
            shape((lon, 128), F32),
            shape((256, 128), BF),
        ),
        [pltpu.VMEM((lon, COLS), F32), pltpu.VMEM((2, 128, lon), F32)],
    )(sea_coupling_matrix, angle_parts, own_sea, own_damp, *others)

    got = got.reshape(BANDS, FIELDS, 5, 8, 128).transpose(2, 1, 0, 3, 4).reshape(5, FIELDS, 256, 128)
    partner = lax.ppermute(got[2:], "band", [(i, i ^ 1) for i in range(BANDS)])
    out = call(
        atmosphere_kernel,
        vmem(5),
        shape((WAVES, OUT_ROWS, 128), BF),
        [
            pltpu.VMEM((NLAT // 128, NPAIR * 8, 128), F32),
            pltpu.VMEM((ITEMS * 8, NLAT), F32),
            pltpu.VMEM((LO, 128, 256), F32),
            pltpu.VMEM((2, 128, NLAT), BF),
            pltpu.VMEM((NLAT // 128, STEPS * 8, 128), F32),
            pltpu.VMEM((NLAT, BANDS * SLOTS), BF),
        ],
    )(got, partner, select_x, select_end, operator)

    back = lax.all_to_all(out, AXES, 0, 0, tiled=True)
    flux_in = back[:, :24].reshape(WAVES, 2, STEPS, 128).transpose(2, 1, 0, 3).reshape(STEPS, COLS, 128)
    sea_end, ocean_coef = call(
        ocean_kernel,
        vmem(6),
        (shape((SLOTS, lon), F32), shape((STEPS * SLOTS, COLS), BF)),
        [
            pltpu.VMEM((lon, 128), F32),
            pltpu.VMEM((lon, COLS), BF),
            pltpu.VMEM((lon, COLS), F32),
            pltpu.VMEM((STEPS * SLOTS, COLS), F32),
            pltpu.VMEM((2, 128, COLS), F32),
        ],
    )(flux_in, zonal_t, zonal, couple, ocean0, shrink)
    ocean_coef = ocean_coef.reshape(STEPS, SLOTS, COLS)
    air_coefficients_end = call(
        unpack_kernel,
        vmem(1),
        shape((LEVELS * LAT, COLS), F32),
        [pltpu.VMEM((WAVES * 16, 128), F32), pltpu.VMEM((2, LEVELS * LAT, 128), F32)],
    )(back).reshape(1, LEVELS, LAT, COLS)

    up = [(i, i + 1) for i in range(BANDS - 1)]
    down = [(j, i) for i, j in up]
    before = lax.ppermute(ocean_coef, "band", up)
    after = lax.ppermute(ocean_coef, "band", down)
    neighbours = jnp.concatenate([before, ocean_coef, after], axis=1)
    slot_index = jnp.arange(3 * SLOTS, dtype=jnp.int32)[None, :]
    first = (air_paired_cells[0] - (band - 1) * SLOTS)[:, None]
    second = (air_paired_cells[1] - (band - 1) * SLOTS)[:, None]
    return_taps = jnp.where(slot_index == first, (1.0 - air_second_share)[:, None], 0.0) + jnp.where(
        slot_index == second, air_second_share[:, None], 0.0
    )
    skin_heat_newest = jnp.einsum(
        "ga,kac->kgc", return_taps.astype(BF), neighbours, preferred_element_type=F32
    )[:, None]
    return (air_coefficients_end, sea_end[None], skin_heat_newest)


def solution(mesh):
    return jax.shard_map(
        per_device,
        mesh=mesh,
        in_specs=(
            P("lev", None, "band", None),
            P("band"),
            P("band", None, None),
            P(),
            P("lev", None, None, "band"),
            P("lev", "band"),
            P(None, "lev", "band", None),
            P("lev", "band", None),
            P("lev", "band", None),
            P(),
            P("band"),
            P("band"),
            P("band"),
            P(None, "band"),
            P("band"),
        ),
        out_specs=(
            P("lev", None, "band", None),
            P("lev", "band", None),
            P(None, "lev", "band", None),
        ),
        check_vma=False,
    )
```

```python
import math

import jax
import jax.numpy as jnp
import numpy as np
from jax import lax
from jax.experimental import pallas as pl
from jax.experimental.pallas import tpu as pltpu
from jax.sharding import PartitionSpec as P


MARG = 8
AXES = ("band", "lev")
degree_damping = 2e-06
ocean_step = 0.5
mixing_diagonal = 0.95
synth_divisor = 4.0

BANDS, FIELDS = 32, 4
LEVELS, LAT, COLS = 16, 40, 256
NLAT = BANDS * LAT
WAVES = COLS // 2
STEPS = 12
SLOTS = 32
LO = LAT // 8
ITEMS = 32
PAIRS = [(l, p) for l in range(LEVELS) for p in range(l + 1, LEVELS)]
NPAIR = len(PAIRS)
XROWS = 24
OUT_ROWS = 40
CHUNK = XROWS + 16
BF = jnp.bfloat16
F32 = jnp.float32
NT = (((1,), (1,)), ((), ()))


def pair_matrix():
    q = np.zeros((LEVELS * LEVELS, 128), np.float32)
    for i, (l, p) in enumerate(PAIRS):
        q[l * LEVELS + p, i] = 1.0
        q[p * LEVELS + l, i] = -1.0
    return q


def hi_lo(v):
    hi = v.astype(BF)
    return hi, (v - hi.astype(F32)).astype(BF)


def position():
    return lax.axis_index("band"), lax.axis_index("lev")


def split_columns():
    row = lax.broadcasted_iota(jnp.int32, (COLS, COLS), 0)
    col = lax.broadcasted_iota(jnp.int32, (COLS, COLS), 1)
    return jnp.where(row == 2 * (col % WAVES) + col // WAVES, 1.0, 0.0).astype(BF)


def join_columns():
    row = lax.broadcasted_iota(jnp.int32, (COLS, COLS), 0)
    col = lax.broadcasted_iota(jnp.int32, (COLS, COLS), 1)
    return jnp.where(col == 2 * (row % WAVES) + row // WAVES, 1.0, 0.0).astype(BF)


def block_transpose(arrays, width):
    arrays = list(arrays)
    block = lax.broadcasted_iota(jnp.int32, arrays[0].shape, 1) // width
    s = 1
    while s < len(arrays):
        upper = (block & s) != 0
        for i in range(len(arrays)):
            if not i & s:
                a, b = arrays[i], arrays[i | s]
                arrays[i] = jnp.where(upper, pltpu.roll(b, s * width, 1), a)
                arrays[i | s] = jnp.where(upper, b, pltpu.roll(a, 128 - s * width, 1))
        s *= 2
    return arrays


def pack_kernel(live_ref, x_ref, s_ref, b_ref, w_ref, k_ref, south_ref, north_ref, q_ref, o_ref, d_ref, t_ref):
    ids = position()
    spread = split_columns()
    base = 0
    for ref in (x_ref, s_ref):
        n = ref.shape[0]
        d = jnp.dot(ref[...].astype(BF), spread, preferred_element_type=F32)
        d_ref[0, base : base + n, :] = d[:, :WAVES]
        d_ref[1, base : base + n, :] = d[:, WAVES:]
        base += n
    slot = lax.broadcasted_iota(jnp.int32, (1, SLOTS), 1)
    live = slot < live_ref[0]
    offset = (south_ref[...] - (ids[0] * LAT - MARG)).astype(F32)
    low = jnp.where(live, 1.0 - north_ref[...], 0.0)
    high = jnp.where(live, north_ref[...], 0.0)
    kind = jnp.full((1, SLOTS), ids[1], jnp.int32)
    taps = jnp.where(kind == 0, offset, jnp.where(kind == 1, low, high))
    taps = jnp.concatenate([taps, jnp.zeros((1, LAT - SLOTS), F32)], axis=1)
    w_hi, w_lo = hi_lo(w_ref[...])
    k_hi, k_lo = hi_lo(k_ref[...])
    rows = [w_hi.astype(F32), w_lo.astype(F32), k_hi.astype(F32), k_lo.astype(F32), taps]
    small = jnp.concatenate(rows + [jnp.zeros((3, LAT), F32)], axis=0).T
    for c in range(2):
        for i, pick in enumerate((c, 2 + c, 4)):
            d_ref[c, (28 + i) * LAT : (29 + i) * LAT, :] = jnp.broadcast_to(
                small[:, pick : pick + 1], (LAT, WAVES)
            )
        d_ref[c, 31 * LAT : 32 * LAT, :] = jnp.zeros((LAT, WAVES), F32)
    m_hi, m_lo = hi_lo(b_ref[...].T)
    mix = jnp.dot(m_hi, q_ref[...], preferred_element_type=F32)
    mix = mix + jnp.dot(m_lo, q_ref[...], preferred_element_type=F32)
    for j in range(XROWS // 8):
        for h in range(8):
            parts = []
            for q in range(2):
                for c in range(2):
                    lo = 2 * j + q
                    if lo < LO:
                        parts.append(d_ref[c, pl.ds(lo * 8 + h, ITEMS, stride=LAT), :])
                    else:
                        parts.append(jnp.zeros((ITEMS, WAVES), F32))
            t_ref[pl.ds(j * 8 + h, WAVES, stride=XROWS), :] = jnp.concatenate(parts, axis=0).T

    upper = lax.broadcasted_iota(jnp.int32, (8, 128), 1) >= 64
    for core in range(2):
        half = mix[32:40] if core else pltpu.roll(mix[32:40], 64, 1)
        spare = jnp.concatenate([jnp.zeros((16, 128), F32), jnp.where(upper, half, 0.0)], axis=0)
        whole = mix[16 * core : 16 * core + 16].astype(BF)

        def put(j, _):
            m = j // FIELDS * (2 * FIELDS) + core * FIELDS + j % FIELDS
            rows = t_ref[pl.ds(pl.multiple_of(m * XROWS, 8), XROWS), :]
            o_ref[m, 0:XROWS, :] = (rows + spare).astype(BF)
            o_ref[m, XROWS:CHUNK, :] = whole
            return 0

        lax.fori_loop(0, WAVES // 2, put, 0, unroll=8)


def operator_kernel(wave_ref, table_ref, p_ref, t_ref, d_ref, sem):
    ids = position()

    def copy(lo):
        return pltpu.make_async_copy(table_ref.at[ids[1], :, lo], t_ref.at[lo], sem.at[lo])

    for lo in range(LO):
        copy(lo).start()
    degree_count = p_ref.shape[1]
    wave = wave_ref[ids[0] * FIELDS + ids[1]]
    degrees = wave + lax.broadcasted_iota(jnp.int32, (1, degree_count), 1)
    degree_float = degrees.astype(F32)
    damping = 1.0 / (1.0 + degree_damping * degree_float * (degree_float + 1.0))
    damping = jnp.where(degrees < degree_count, damping, 0.0)
    scale = 1.0 / (synth_divisor * math.sqrt(degree_count) * math.sqrt(NLAT))
    for lo in range(LO):
        copy(lo).wait()
        part = t_ref[lo].reshape(BANDS * 8, degree_count)
        d_ref[lo * 256 : (lo + 1) * 256, :] = (part.astype(F32) * damping).astype(BF)
    for lo in range(LO):
        part = t_ref[lo].reshape(BANDS * 8, degree_count)
        p = lax.dot_general(part, d_ref[...], NT, preferred_element_type=F32)
        p_ref[lo * 256 : (lo + 1) * 256, :] = (p * scale).astype(BF)


def tables_kernel(c_ref, a_ref, own_s, own_d, o1, o2, o3, zt_ref, z_ref, so_ref, sr_ref, cp_ref, w_ref, h_ref):
    ids = position()
    lon = own_s.shape[1]
    fine = a_ref[0:80, :]
    for q in range(lon // 40):
        ca = a_ref[80 + q : 81 + q, :]
        sa = a_ref[120 + q : 121 + q, :]
        cos = ca * fine[0:40] - sa * fine[40:80]
        sin = sa * fine[0:40] + ca * fine[40:80]
        w_ref[40 * q : 40 * q + 40, 0:WAVES] = cos
        w_ref[40 * q : 40 * q + 40, WAVES:COLS] = -sin
    zt_ref[...] = w_ref[...].astype(BF)
    for x in range(0, lon, 128):
        w = min(128, lon - x)
        for c in range(2):
            z_ref[c * WAVES : (c + 1) * WAVES, x : x + w] = (
                w_ref[x : x + w, c * WAVES : (c + 1) * WAVES].T.astype(BF)
            )
    for j, (sea, damp) in enumerate(
        [(own_s[...], own_d[...])] + [(o[0:SLOTS, :], o[SLOTS:, :]) for o in (o1, o2, o3)]
    ):
        field = (ids[1] + FIELDS - j) % FIELDS
        at = pl.multiple_of(field * SLOTS, SLOTS)
        h_ref[0, pl.ds(at, SLOTS), :] = sea.astype(F32)
        h_ref[1, pl.ds(at, SLOTS), :] = damp.astype(F32)
    for x in range(0, lon, 128):
        w = min(128, lon - x)
        so_ref[x : x + w, :] = h_ref[0, :, x : x + w].T
        sr_ref[x : x + w, :] = 1.0 / (1.0 + ocean_step * h_ref[1, :, x : x + w].T)
    row = lax.broadcasted_iota(jnp.int32, (128, 128), 0)
    col = lax.broadcasted_iota(jnp.int32, (128, 128), 1)
    same = row % SLOTS == col % SLOTS
    couple = jnp.zeros((128, 128), F32)
    for e in range(FIELDS):
        for f in range(FIELDS):
            v = ocean_step * (c_ref[f, e] - c_ref[e, f])
            couple = jnp.where(same & (row // SLOTS == e) & (col // SLOTS == f), v, couple)
    hi, lo = hi_lo(couple)
    cp_ref[0:128, :] = hi
    cp_ref[128:256, :] = lo


def atmosphere_kernel(
    g_ref, h_any, sx_ref, se_any, p_any, o_ref,
    a_ref, x_ref, y_ref, s_ref, f_ref, t_ref, h_ref, se_ref, p_ref, sem,
):
    copies = [
        pltpu.make_async_copy(src, dst, sem.at[i])
        for i, (src, dst) in enumerate(((h_any, h_ref), (p_any, p_ref), (se_any, se_ref)))
    ]
    for copy in copies:
        copy.start()
    first = position()[0] % 2 == 0
    eye = (
        lax.broadcasted_iota(jnp.int32, (128, 128), 0) == lax.broadcasted_iota(jnp.int32, (128, 128), 1)
    ).astype(F32).astype(BF)
    for lo in range(LO):
        lanes = slice(lo * 256, (lo + 1) * 256)
        rows = jnp.concatenate([g_ref[lo // 2, f] for f in range(FIELDS)], axis=1)
        x_ref[:, lanes] = lax.dot_general(sx_ref[lo % 2], rows, NT, preferred_element_type=F32)

    nslot = BANDS * SLOTS
    slot = lax.broadcasted_iota(jnp.int32, (1, nslot), 1)
    south = x_ref[240:241, 0:nslot] + (slot % 256 // 8 * LAT - MARG).astype(F32)
    low = x_ref[242:243, 0:nslot]
    high = x_ref[244:245, 0:nslot]
    for lo in range(LO):
        r = lax.broadcasted_iota(jnp.int32, (256, 1), 0)
        place = (r // 8 * LAT + lo * 8 + r % 8).astype(F32)
        for col in range(0, nslot, 128):
            at, zero = (0, 144) if col % 256 == 0 else (112, 0)
            lanes = slice(col, col + 128)
            part = place[at : at + 144]
            t_ref[lo * 256 + at : lo * 256 + at + 144, lanes] = jnp.where(
                part == south[:, lanes],
                low[:, lanes],
                jnp.where(part == south[:, lanes] + 1.0, high[:, lanes], 0.0),
            ).astype(BF)
            t_ref[lo * 256 + zero : lo * 256 + zero + 112, lanes] = jnp.zeros((112, 128), BF)

    copies[0].wait()
    for lo in range(LO):
        for f in range(FIELDS):
            if lo < 4:
                own, other = g_ref[3 + lo % 2, f], h_ref[1 + lo % 2, f]
                mix = jnp.where(first == (lo < 2), own, other)
            else:
                own, other = g_ref[2, f].astype(F32), h_ref[0, f].astype(F32)
                lower = lax.broadcasted_iota(jnp.int32, own.shape, 1) < 64
                even = pltpu.roll(jnp.where(first, own, other), 64, 1)
                mix = jnp.where(lower, even, jnp.where(first, other, own)).astype(BF)
            turned = lax.dot_general(eye, mix, NT, preferred_element_type=F32)
            for half in range(2):
                for c in range(2):
                    a_ref[2 * lo + half, pl.ds(2 * f + c, NPAIR, stride=8), :] = turned[
                        0:NPAIR, half * 128 : half * 128 + 128
                    ]

    copies[1].wait()
    copies[2].wait()
    weight = x_ref[28 * 8 : 29 * 8, :]
    for l in range(0, LEVELS, 2):
        pair = x_ref[8 * l : 8 * l + 16, :].reshape(2, 8, NLAT) * weight[None]
        s_ref[0, 8 * l : 8 * l + 16, :] = pair.reshape(16, NLAT).astype(BF)

    def mix_block(k, n, half):
        lanes = slice(n * 256 + half * 128, n * 256 + half * 128 + 128)
        mid = [
            x_ref[8 * l : 8 * l + 8, lanes] - y_ref[n, 8 * l : 8 * l + 8, half * 128 : half * 128 + 128]
            for l in range(LEVELS)
        ]
        skin = x_ref[pl.ds(pl.multiple_of(128 + 8 * k, 8), 8), lanes]
        flux = x_ref[29 * 8 : 30 * 8, lanes] * (skin - mid[LEVELS - 1])
        f_ref[2 * n + half, pl.ds(k, 8, stride=STEPS), :] = flux
        acc = [mixing_diagonal * v for v in mid]
        acc[LEVELS - 1] = acc[LEVELS - 1] + flux
        for i, (l, p) in enumerate(PAIRS):
            a = a_ref[2 * n + half, 8 * i : 8 * i + 8, :]
            acc[l] = acc[l] + a * mid[p]
            acc[p] = acc[p] - a * mid[l]
        scale = x_ref[28 * 8 : 29 * 8, lanes]
        for l in range(LEVELS):
            x_ref[8 * l : 8 * l + 8, lanes] = acc[l]
        for l in range(0, LEVELS, 2):
            pair = jnp.concatenate([acc[l] * scale, acc[l + 1] * scale], axis=0)
            s_ref[1 - k % 2, 8 * l : 8 * l + 16, lanes] = pair.astype(BF)

    def step(k, _):
        for n in range(LO + 1):
            if n < LO:
                y_ref[n] = jnp.dot(
                    s_ref[k % 2], p_ref[:, n * 256 : (n + 1) * 256], preferred_element_type=F32
                )
            if n > 0:
                mix_block(k, n - 1, 0)
                mix_block(k, n - 1, 1)
        return 0

    lax.fori_loop(0, STEPS, step, 0)

    flux = jnp.concatenate([f_ref[n].astype(BF) for n in range(NLAT // 128)], axis=1)
    at_slots = jnp.dot(flux, t_ref[...], preferred_element_type=F32) * (-ocean_step / math.sqrt(COLS))
    ends = jnp.concatenate(
        [x_ref[0:128, n * 128 : (n + 1) * 128].T.astype(BF) for n in range(NLAT // 128)], axis=0
    )
    ends = jnp.concatenate([ends[lo * 256 : (lo + 1) * 256] for lo in range(LO)], axis=1)
    ends = jnp.dot(ends, se_ref[...], preferred_element_type=F32)
    for u in range(2):
        pieces = []
        for f in range(FIELDS):
            for s in range(4):
                at = s * 256 + u * 128
                pieces.append(at_slots[f * 24 : f * 24 + 24, at : at + 128])
        for i, v in enumerate(block_transpose(pieces, 8)):
            tile = u * 16 + i
            for f in range(FIELDS):
                o_ref[tile * FIELDS + f, 0:24, :] = v.astype(BF)
    for b in range(BANDS):
        for f in range(FIELDS):
            pair = [ends[8 * b : 8 * b + 8, (q * FIELDS + f) * 128 : (q * FIELDS + f + 1) * 128] for q in range(2)]
            o_ref[b * FIELDS + f, 24:40, :] = jnp.concatenate(pair, axis=0).astype(BF)


def ocean_kernel(
    f_ref, zt_ref, z_any, c_ref, o0_any, r_any, so_ref, co_ref,
    o_ref, w_ref, p_ref, t_ref, h_ref, z_ref, r_ref, sem,
):
    lon = o_ref.shape[0]
    start = pl.multiple_of(position()[1] * SLOTS, SLOTS)
    copies = [
        pltpu.make_async_copy(src, dst, sem.at[i])
        for i, (src, dst) in enumerate(((o0_any, o_ref), (r_any, r_ref), (z_any, z_ref)))
    ]
    for copy in copies:
        copy.start()

    def push(j, slot):
        pair = jnp.concatenate([f_ref[2 * j], f_ref[2 * j + 1]], axis=1)
        p_ref[slot] = jnp.dot(zt_ref[...], pair, preferred_element_type=F32)

    scale = 1.0 / math.sqrt(lon)

    def two_steps(j, _):
        for i in range(2):
            coarse = o_ref[...].astype(BF)
            pull = jnp.dot(
                jnp.concatenate([coarse, coarse], axis=1), c_ref[...], preferred_element_type=F32
            )
            updated = (o_ref[...] + (pull + p_ref[j % 2, :, i * 128 : (i + 1) * 128])) * r_ref[...]
            o_ref[...] = updated
            w_ref[:, i * 128 : (i + 1) * 128] = updated.astype(BF)
        push(jnp.minimum(j + 1, STEPS // 2 - 1), (j + 1) % 2)
        coef = jnp.dot(z_ref[...], w_ref[...], preferred_element_type=F32) * scale
        for i in range(2):
            h_ref[i] = coef[:, i * 128 : (i + 1) * 128].T
            at = pl.multiple_of((2 * j + i) * SLOTS, SLOTS)
            t_ref[pl.ds(at, SLOTS), :] = h_ref[i, pl.ds(start, SLOTS), :]
        return 0

    push(0, 0)
    for copy in copies:
        copy.wait()
    lax.fori_loop(0, STEPS // 2, two_steps, 0)
    co_ref[...] = jnp.dot(t_ref[...].astype(BF), join_columns(), preferred_element_type=F32).astype(BF)
    for x in range(0, lon, 128):
        w = min(128, lon - x)
        h_ref[0, :, 0:w] = o_ref[x : x + w, :].T
        so_ref[:, x : x + w] = h_ref[0, pl.ds(start, SLOTS), 0:w]


def unpack_kernel(b_any, o_ref, t_ref, v_ref, b_ref, sem):
    copy = pltpu.make_async_copy(b_any.at[:, 24:40, :], b_ref, sem)
    copy.start()
    copy.wait()

    def take(m, _):
        t_ref[pl.ds(pl.multiple_of(m * 16, 16), 16), :] = b_ref[m].astype(F32)
        return 0

    lax.fori_loop(0, WAVES, take, 0, unroll=8)
    for q in range(2):
        for h in range(8):
            v = t_ref[pl.ds(q * 8 + h, WAVES, stride=16), :].T
            for i in range(4 if q == 0 else 1):
                for c in range(2):
                    at = i * 32 + c * LEVELS
                    v_ref[c, pl.ds((4 * q + i) * 8 + h, LEVELS, stride=LAT), :] = v[at : at + LEVELS]
    both = jnp.concatenate([v_ref[0], v_ref[1]], axis=1).astype(BF)
    o_ref[...] = jnp.dot(both, join_columns(), preferred_element_type=F32)


def vmem(n):
    return [pl.BlockSpec(memory_space=pltpu.VMEM)] * n


def anywhere(n):
    return [pl.BlockSpec(memory_space=pl.ANY)] * n


def smem(n):
    return [pl.BlockSpec(memory_space=pltpu.SMEM)] * n


def call(kernel, in_specs, out_shape, scratch):
    return pl.pallas_call(
        kernel,
        out_shape=out_shape,
        in_specs=in_specs,
        out_specs=jax.tree.map(lambda _: pl.BlockSpec(memory_space=pltpu.VMEM), out_shape),
        scratch_shapes=scratch,
    )


def shape(dims, kind):
    return jax.ShapeDtypeStruct(dims, kind)


def state_selection():
    col = jnp.arange(FIELDS * 128, dtype=jnp.int32)[None, :]
    row = jnp.arange(ITEMS * 8, dtype=jnp.int32)[:, None]
    item = row // 8
    same = (col % ITEMS == item) & (col // 128 == row % 8 // 2)
    same_c = (col % 64 // ITEMS == row % 2) | (item == 28) | (item == 29)
    return jnp.stack([same & same_c & (col % 128 // 64 == q) for q in range(2)]).astype(BF)


def end_selection():
    row = jnp.arange(LO * 128, dtype=jnp.int32)[:, None]
    col = jnp.arange(2 * FIELDS * 128, dtype=jnp.int32)[None, :]
    lo = col // 512 * 4 + col % 128 // 32
    at = lo * 128 + col % LEVELS * 8 + col % 512 // 128 * 2 + col % 32 // LEVELS
    return (row == at).astype(BF)


def per_device(
    air_fourier_coefficients,
    quadrature_factor,
    associated_polynomial_table,
    east_west_harmonic,
    boundary_diffusion,
    bulk_transfer_coefficient,
    skin_heat_earlier,
    sea_boundary_values,
    sea_damping_speed,
    sea_coupling_matrix,
    patch_active_entries,
    sea_southern_parallel,
    sea_northern_share,
    air_paired_cells,
    air_second_share,
):
    band = lax.axis_index("band")
    lon = sea_boundary_values.shape[2]
    degree_count = associated_polynomial_table.shape[2]

    chunks = call(
        pack_kernel,
        smem(1) + vmem(8),
        shape((WAVES, CHUNK, 128), BF),
        [pltpu.VMEM((2, ITEMS * LAT, 128), F32), pltpu.VMEM((WAVES * XROWS, 128), F32)],
    )(
        patch_active_entries,
        air_fourier_coefficients.reshape(LEVELS * LAT, COLS),
        skin_heat_earlier.reshape(STEPS * LAT, COLS),
        boundary_diffusion.reshape(LEVELS * LEVELS, LAT),
        quadrature_factor[None],
        bulk_transfer_coefficient,
        sea_southern_parallel[None],
        sea_northern_share[None],
        jnp.asarray(pair_matrix(), BF),
    )
    got = lax.all_to_all(chunks, AXES, 0, 0, tiled=True)

    operator = call(
        operator_kernel,
        smem(1) + [pl.BlockSpec(memory_space=pl.ANY)],
        shape((NLAT, NLAT), BF),
        [
            pltpu.VMEM((LO, BANDS, 8, degree_count), BF),
            pltpu.VMEM((NLAT, degree_count), BF),
            pltpu.SemaphoreType.DMA((LO,)),
        ],
    )(east_west_harmonic, associated_polynomial_table.reshape(FIELDS, BANDS, LO, 8, degree_count))

    select_x = state_selection()
    select_end = end_selection()

    part = jnp.arange(160, dtype=jnp.int32)[:, None]
    longitude = jnp.where(part < 80, part % 40, part % 40 * 40)
    phases = longitude * east_west_harmonic[None, :] % lon
    angles = phases.astype(F32) * (2.0 * math.pi / lon)
    angle_parts = jnp.where(part // 40 % 2 == 0, jnp.cos(angles), jnp.sin(angles))
    own_sea, own_damp = sea_boundary_values[0], sea_damping_speed[0]
    sent = jnp.concatenate([own_sea.astype(BF), own_damp.astype(BF)], axis=0)
    others = []
    for d in range(1, FIELDS):
        others.append(lax.ppermute(sent, "lev", [(i, (i + d) % FIELDS) for i in range(FIELDS)]))
    zonal_t, zonal, ocean0, shrink, couple = call(
        tables_kernel,
        smem(1) + vmem(6),
        (
            shape((lon, COLS), BF),
            shape((COLS, lon), BF),
            shape((lon, 128), F32),
            shape((lon, 128), F32),
            shape((256, 128), BF),
        ),
        [pltpu.VMEM((lon, COLS), F32), pltpu.VMEM((2, 128, lon), F32)],
    )(sea_coupling_matrix, angle_parts, own_sea, own_damp, *others)

    got = got.reshape(BANDS, FIELDS, 5, 8, 128).transpose(2, 1, 0, 3, 4).reshape(5, FIELDS, 256, 128)
    partner = lax.ppermute(got[2:], "band", [(i, i ^ 1) for i in range(BANDS)])
    out = call(
        atmosphere_kernel,
        vmem(1) + anywhere(1) + vmem(1) + anywhere(2),
        shape((WAVES, OUT_ROWS, 128), BF),
        [
            pltpu.VMEM((NLAT // 128, NPAIR * 8, 128), F32),
            pltpu.VMEM((ITEMS * 8, NLAT), F32),
            pltpu.VMEM((LO, 128, 256), F32),
            pltpu.VMEM((2, 128, NLAT), BF),
            pltpu.VMEM((NLAT // 128, STEPS * 8, 128), F32),
            pltpu.VMEM((NLAT, BANDS * SLOTS), BF),
            pltpu.VMEM((3, FIELDS, 256, 128), BF),
            pltpu.VMEM((LO * 128, 1024), BF),
            pltpu.VMEM((NLAT, NLAT), BF),
            pltpu.SemaphoreType.DMA((3,)),
        ],
    )(got, partner, select_x, select_end, operator)

    back = lax.all_to_all(out, AXES, 0, 0, tiled=True)
    flux_in = back[:, :24].reshape(WAVES, 2, STEPS, 128).transpose(2, 1, 0, 3).reshape(STEPS, COLS, 128)
    sea_end, ocean_coef = call(
        ocean_kernel,
        vmem(2) + anywhere(1) + vmem(1) + anywhere(2),
        (shape((SLOTS, lon), F32), shape((STEPS * SLOTS, COLS), BF)),
        [
            pltpu.VMEM((lon, 128), F32),
            pltpu.VMEM((lon, COLS), BF),
            pltpu.VMEM((2, lon, COLS), F32),
            pltpu.VMEM((STEPS * SLOTS, COLS), F32),
            pltpu.VMEM((2, 128, COLS), F32),
            pltpu.VMEM((COLS, lon), BF),
            pltpu.VMEM((lon, 128), F32),
            pltpu.SemaphoreType.DMA((3,)),
        ],
    )(flux_in, zonal_t, zonal, couple, ocean0, shrink)
    ocean_coef = ocean_coef.reshape(STEPS, SLOTS, COLS)
    air_coefficients_end = call(
        unpack_kernel,
        anywhere(1),
        shape((LEVELS * LAT, COLS), F32),
        [
            pltpu.VMEM((WAVES * 16, 128), F32),
            pltpu.VMEM((2, LEVELS * LAT, 128), F32),
            pltpu.VMEM((WAVES, 16, 128), BF),
            pltpu.SemaphoreType.DMA,
        ],
    )(back).reshape(1, LEVELS, LAT, COLS)

    up = [(i, i + 1) for i in range(BANDS - 1)]
    down = [(j, i) for i, j in up]
    before = lax.ppermute(ocean_coef, "band", up)
    after = lax.ppermute(ocean_coef, "band", down)
    neighbours = jnp.concatenate([before, ocean_coef, after], axis=1)
    slot_index = jnp.arange(3 * SLOTS, dtype=jnp.int32)[None, :]
    first = (air_paired_cells[0] - (band - 1) * SLOTS)[:, None]
    second = (air_paired_cells[1] - (band - 1) * SLOTS)[:, None]
    return_taps = jnp.where(slot_index == first, (1.0 - air_second_share)[:, None], 0.0) + jnp.where(
        slot_index == second, air_second_share[:, None], 0.0
    )
    skin_heat_newest = jnp.einsum(
        "ga,kac->kgc", return_taps.astype(BF), neighbours, preferred_element_type=F32
    )[:, None]
    return (air_coefficients_end, sea_end[None], skin_heat_newest)


def solution(mesh):
    return jax.shard_map(
        per_device,
        mesh=mesh,
        in_specs=(
            P("lev", None, "band", None),
            P("band"),
            P("band", None, None),
            P(),
            P("lev", None, None, "band"),
            P("lev", "band"),
            P(None, "lev", "band", None),
            P("lev", "band", None),
            P("lev", "band", None),
            P(),
            P("band"),
            P("band"),
            P("band"),
            P(None, "band"),
            P("band"),
        ),
        out_specs=(
            P("lev", None, "band", None),
            P("lev", "band", None),
            P(None, "lev", "band", None),
        ),
        check_vma=False,
    )
```

```python
import math

import jax
import jax.numpy as jnp
import numpy as np
from jax import lax
from jax.experimental import pallas as pl
from jax.experimental.pallas import tpu as pltpu
from jax.sharding import PartitionSpec as P


MARG = 8
AXES = ("band", "lev")
degree_damping = 2e-06
ocean_step = 0.5
mixing_diagonal = 0.95
synth_divisor = 4.0

BANDS, FIELDS = 32, 4
LEVELS, LAT, COLS = 16, 40, 256
NLAT = BANDS * LAT
WAVES = COLS // 2
STEPS = 12
SLOTS = 32
LO = LAT // 8
ITEMS = 32
PAIRS = [(l, p) for l in range(LEVELS) for p in range(l + 1, LEVELS)]
NPAIR = len(PAIRS)
XROWS = 24
OUT_ROWS = 40
CHUNK = XROWS + 16
BF = jnp.bfloat16
F32 = jnp.float32
NT = (((1,), (1,)), ((), ()))


def pair_matrix():
    q = np.zeros((LEVELS * LEVELS, 128), np.float32)
    for i, (l, p) in enumerate(PAIRS):
        q[l * LEVELS + p, i] = 1.0
        q[p * LEVELS + l, i] = -1.0
    return q


def hi_lo(v):
    hi = v.astype(BF)
    return hi, (v - hi.astype(F32)).astype(BF)


def position():
    return lax.axis_index("band"), lax.axis_index("lev")


def split_columns():
    row = lax.broadcasted_iota(jnp.int32, (COLS, COLS), 0)
    col = lax.broadcasted_iota(jnp.int32, (COLS, COLS), 1)
    return jnp.where(row == 2 * (col % WAVES) + col // WAVES, 1.0, 0.0).astype(BF)


def join_columns():
    row = lax.broadcasted_iota(jnp.int32, (COLS, COLS), 0)
    col = lax.broadcasted_iota(jnp.int32, (COLS, COLS), 1)
    return jnp.where(col == 2 * (row % WAVES) + row // WAVES, 1.0, 0.0).astype(BF)


def block_transpose(arrays, width):
    arrays = list(arrays)
    block = lax.broadcasted_iota(jnp.int32, arrays[0].shape, 1) // width
    s = 1
    while s < len(arrays):
        upper = (block & s) != 0
        for i in range(len(arrays)):
            if not i & s:
                a, b = arrays[i], arrays[i | s]
                arrays[i] = jnp.where(upper, pltpu.roll(b, s * width, 1), a)
                arrays[i | s] = jnp.where(upper, b, pltpu.roll(a, 128 - s * width, 1))
        s *= 2
    return arrays


def pack_kernel(live_ref, x_ref, s_ref, b_ref, w_ref, k_ref, south_ref, north_ref, q_ref, o_ref, d_ref, t_ref):
    ids = position()
    spread = split_columns()
    base = 0
    for ref in (x_ref, s_ref):
        n = ref.shape[0]
        d = jnp.dot(ref[...].astype(BF), spread, preferred_element_type=F32)
        d_ref[0, base : base + n, :] = d[:, :WAVES]
        d_ref[1, base : base + n, :] = d[:, WAVES:]
        base += n
    slot = lax.broadcasted_iota(jnp.int32, (1, SLOTS), 1)
    live = slot < live_ref[0]
    offset = (south_ref[...] - (ids[0] * LAT - MARG)).astype(F32)
    low = jnp.where(live, 1.0 - north_ref[...], 0.0)
    high = jnp.where(live, north_ref[...], 0.0)
    kind = jnp.full((1, SLOTS), ids[1], jnp.int32)
    taps = jnp.where(kind == 0, offset, jnp.where(kind == 1, low, high))
    taps = jnp.concatenate([taps, jnp.zeros((1, LAT - SLOTS), F32)], axis=1)
    w_hi, w_lo = hi_lo(w_ref[...])
    k_hi, k_lo = hi_lo(k_ref[...])
    rows = [w_hi.astype(F32), w_lo.astype(F32), k_hi.astype(F32), k_lo.astype(F32), taps]
    small = jnp.concatenate(rows + [jnp.zeros((3, LAT), F32)], axis=0).T
    for c in range(2):
        for i, pick in enumerate((c, 2 + c, 4)):
            d_ref[c, (28 + i) * LAT : (29 + i) * LAT, :] = jnp.broadcast_to(
                small[:, pick : pick + 1], (LAT, WAVES)
            )
        d_ref[c, 31 * LAT : 32 * LAT, :] = jnp.zeros((LAT, WAVES), F32)
    m_hi, m_lo = hi_lo(b_ref[...].T)
    mix = jnp.dot(m_hi, q_ref[...], preferred_element_type=F32)
    mix = mix + jnp.dot(m_lo, q_ref[...], preferred_element_type=F32)
    for j in range(XROWS // 8):
        for h in range(8):
            parts = []
            for q in range(2):
                for c in range(2):
                    lo = 2 * j + q
                    if lo < LO:
                        parts.append(d_ref[c, pl.ds(lo * 8 + h, ITEMS, stride=LAT), :])
                    else:
                        parts.append(jnp.zeros((ITEMS, WAVES), F32))
            t_ref[pl.ds(j * 8 + h, WAVES, stride=XROWS), :] = jnp.concatenate(parts, axis=0).T

    upper = lax.broadcasted_iota(jnp.int32, (8, 128), 1) >= 64
    for core in range(2):
        half = mix[32:40] if core else pltpu.roll(mix[32:40], 64, 1)
        spare = jnp.concatenate([jnp.zeros((16, 128), F32), jnp.where(upper, half, 0.0)], axis=0)
        whole = mix[16 * core : 16 * core + 16].astype(BF)

        def put(j, _):
            m = j // FIELDS * (2 * FIELDS) + core * FIELDS + j % FIELDS
            rows = t_ref[pl.ds(pl.multiple_of(m * XROWS, 8), XROWS), :]
            o_ref[m, 0:XROWS, :] = (rows + spare).astype(BF)
            o_ref[m, XROWS:CHUNK, :] = whole
            return 0

        lax.fori_loop(0, WAVES // 2, put, 0, unroll=16)


def operator_kernel(wave_ref, table_ref, p_ref, t_ref, d_ref, sem):
    ids = position()

    def copy(lo):
        return pltpu.make_async_copy(table_ref.at[ids[1], :, lo], t_ref.at[lo], sem.at[lo])

    for lo in range(LO):
        copy(lo).start()
    degree_count = p_ref.shape[1]
    wave = wave_ref[ids[0] * FIELDS + ids[1]]
    degrees = wave + lax.broadcasted_iota(jnp.int32, (1, degree_count), 1)
    degree_float = degrees.astype(F32)
    damping = 1.0 / (1.0 + degree_damping * degree_float * (degree_float + 1.0))
    damping = jnp.where(degrees < degree_count, damping, 0.0)
    scale = 1.0 / (synth_divisor * math.sqrt(degree_count) * math.sqrt(NLAT))
    for lo in range(LO):
        copy(lo).wait()
        part = t_ref[lo].reshape(BANDS * 8, degree_count)
        d_ref[lo * 256 : (lo + 1) * 256, :] = (part.astype(F32) * damping).astype(BF)
    for lo in range(LO):
        part = t_ref[lo].reshape(BANDS * 8, degree_count)
        p = lax.dot_general(part, d_ref[...], NT, preferred_element_type=F32)
        p_ref[lo * 256 : (lo + 1) * 256, :] = (p * scale).astype(BF)


def tables_kernel(c_ref, a_ref, own_s, own_d, o1, o2, o3, zt_ref, z_ref, so_ref, sr_ref, cp_ref, w_ref, h_ref):
    ids = position()
    lon = own_s.shape[1]
    fine = a_ref[0:80, :]
    for q in range(lon // 40):
        ca = a_ref[80 + q : 81 + q, :]
        sa = a_ref[120 + q : 121 + q, :]
        cos = ca * fine[0:40] - sa * fine[40:80]
        sin = sa * fine[0:40] + ca * fine[40:80]
        w_ref[40 * q : 40 * q + 40, 0:WAVES] = cos
        w_ref[40 * q : 40 * q + 40, WAVES:COLS] = -sin
    zt_ref[...] = w_ref[...].astype(BF)
    for x in range(0, lon, 128):
        w = min(128, lon - x)
        for c in range(2):
            z_ref[c * WAVES : (c + 1) * WAVES, x : x + w] = (
                w_ref[x : x + w, c * WAVES : (c + 1) * WAVES].T.astype(BF)
            )
    for j, (sea, damp) in enumerate(
        [(own_s[...], own_d[...])] + [(o[0:SLOTS, :], o[SLOTS:, :]) for o in (o1, o2, o3)]
    ):
        field = (ids[1] + FIELDS - j) % FIELDS
        at = pl.multiple_of(field * SLOTS, SLOTS)
        h_ref[0, pl.ds(at, SLOTS), :] = sea.astype(F32)
        h_ref[1, pl.ds(at, SLOTS), :] = damp.astype(F32)
    for x in range(0, lon, 128):
        w = min(128, lon - x)
        so_ref[x : x + w, :] = h_ref[0, :, x : x + w].T
        sr_ref[x : x + w, :] = 1.0 / (1.0 + ocean_step * h_ref[1, :, x : x + w].T)
    row = lax.broadcasted_iota(jnp.int32, (128, 128), 0)
    col = lax.broadcasted_iota(jnp.int32, (128, 128), 1)
    same = row % SLOTS == col % SLOTS
    couple = jnp.zeros((128, 128), F32)
    for e in range(FIELDS):
        for f in range(FIELDS):
            v = ocean_step * (c_ref[f, e] - c_ref[e, f])
            couple = jnp.where(same & (row // SLOTS == e) & (col // SLOTS == f), v, couple)
    hi, lo = hi_lo(couple)
    cp_ref[0:128, :] = hi
    cp_ref[128:256, :] = lo


def atmosphere_kernel(
    g_ref, h_any, sx_ref, se_any, p_any, o_ref,
    a_ref, x_ref, y_ref, s_ref, f_ref, t_ref, h_ref, se_ref, p_ref, sem,
):
    copies = [
        pltpu.make_async_copy(src, dst, sem.at[i])
        for i, (src, dst) in enumerate(((h_any, h_ref), (p_any, p_ref), (se_any, se_ref)))
    ]
    for copy in copies:
        copy.start()
    first = position()[0] % 2 == 0
    eye = (
        lax.broadcasted_iota(jnp.int32, (128, 128), 0) == lax.broadcasted_iota(jnp.int32, (128, 128), 1)
    ).astype(F32).astype(BF)
    for lo in range(LO):
        lanes = slice(lo * 256, (lo + 1) * 256)
        rows = jnp.concatenate([g_ref[lo // 2, f] for f in range(FIELDS)], axis=1)
        x_ref[:, lanes] = lax.dot_general(sx_ref[lo % 2], rows, NT, preferred_element_type=F32)

    nslot = BANDS * SLOTS
    slot = lax.broadcasted_iota(jnp.int32, (1, nslot), 1)
    south = x_ref[240:241, 0:nslot] + (slot % 256 // 8 * LAT - MARG).astype(F32)
    low = x_ref[242:243, 0:nslot]
    high = x_ref[244:245, 0:nslot]
    for lo in range(LO):
        r = lax.broadcasted_iota(jnp.int32, (256, 1), 0)
        place = (r // 8 * LAT + lo * 8 + r % 8).astype(F32)
        for col in range(0, nslot, 128):
            at, zero = (0, 144) if col % 256 == 0 else (112, 0)
            lanes = slice(col, col + 128)
            part = place[at : at + 144]
            t_ref[lo * 256 + at : lo * 256 + at + 144, lanes] = jnp.where(
                part == south[:, lanes],
                low[:, lanes],
                jnp.where(part == south[:, lanes] + 1.0, high[:, lanes], 0.0),
            ).astype(BF)
            t_ref[lo * 256 + zero : lo * 256 + zero + 112, lanes] = jnp.zeros((112, 128), BF)

    copies[0].wait()
    for lo in range(LO):
        for f in range(FIELDS):
            if lo < 4:
                own, other = g_ref[3 + lo % 2, f], h_ref[1 + lo % 2, f]
                mix = jnp.where(first == (lo < 2), own, other)
            else:
                own, other = g_ref[2, f].astype(F32), h_ref[0, f].astype(F32)
                lower = lax.broadcasted_iota(jnp.int32, own.shape, 1) < 64
                even = pltpu.roll(jnp.where(first, own, other), 64, 1)
                mix = jnp.where(lower, even, jnp.where(first, other, own)).astype(BF)
            turned = lax.dot_general(eye, mix, NT, preferred_element_type=F32)
            for half in range(2):
                for c in range(2):
                    a_ref[2 * lo + half, pl.ds(2 * f + c, NPAIR, stride=8), :] = turned[
                        0:NPAIR, half * 128 : half * 128 + 128
                    ]

    copies[1].wait()
    weight = x_ref[28 * 8 : 29 * 8, :]
    for l in range(0, LEVELS, 2):
        pair = x_ref[8 * l : 8 * l + 16, :].reshape(2, 8, NLAT) * weight[None]
        s_ref[0, 8 * l : 8 * l + 16, :] = pair.reshape(16, NLAT).astype(BF)

    def mix_block(k, n, half):
        lanes = slice(n * 256 + half * 128, n * 256 + half * 128 + 128)
        mid = [
            x_ref[8 * l : 8 * l + 8, lanes] - y_ref[n, 8 * l : 8 * l + 8, half * 128 : half * 128 + 128]
            for l in range(LEVELS)
        ]
        skin = x_ref[pl.ds(pl.multiple_of(128 + 8 * k, 8), 8), lanes]
        flux = x_ref[29 * 8 : 30 * 8, lanes] * (skin - mid[LEVELS - 1])
        f_ref[2 * n + half, pl.ds(k, 8, stride=STEPS), :] = flux
        acc = [mixing_diagonal * v for v in mid]
        acc[LEVELS - 1] = acc[LEVELS - 1] + flux
        for i, (l, p) in enumerate(PAIRS):
            a = a_ref[2 * n + half, 8 * i : 8 * i + 8, :]
            acc[l] = acc[l] + a * mid[p]
            acc[p] = acc[p] - a * mid[l]
        scale = x_ref[28 * 8 : 29 * 8, lanes]
        for l in range(LEVELS):
            x_ref[8 * l : 8 * l + 8, lanes] = acc[l]
        for l in range(0, LEVELS, 2):
            pair = jnp.concatenate([acc[l] * scale, acc[l + 1] * scale], axis=0)
            s_ref[1 - k % 2, 8 * l : 8 * l + 16, lanes] = pair.astype(BF)

    def step(k, _):
        for n in range(LO + 1):
            if n < LO:
                y_ref[n] = jnp.dot(
                    s_ref[k % 2], p_ref[:, n * 256 : (n + 1) * 256], preferred_element_type=F32
                )
            if n > 0:
                mix_block(k, n - 1, 0)
                mix_block(k, n - 1, 1)
        return 0

    lax.fori_loop(0, STEPS, step, 0)

    flux = jnp.concatenate([f_ref[n].astype(BF) for n in range(NLAT // 128)], axis=1)
    at_slots = jnp.dot(flux, t_ref[...], preferred_element_type=F32) * (-ocean_step / math.sqrt(COLS))
    copies[2].wait()
    ends = jnp.concatenate(
        [x_ref[0:128, n * 128 : (n + 1) * 128].T.astype(BF) for n in range(NLAT // 128)], axis=0
    )
    ends = jnp.concatenate([ends[lo * 256 : (lo + 1) * 256] for lo in range(LO)], axis=1)
    ends = jnp.dot(ends, se_ref[...], preferred_element_type=F32)
    for u in range(2):
        pieces = []
        for f in range(FIELDS):
            for s in range(4):
                at = s * 256 + u * 128
                pieces.append(at_slots[f * 24 : f * 24 + 24, at : at + 128])
        for i, v in enumerate(block_transpose(pieces, 8)):
            tile = u * 16 + i
            for f in range(FIELDS):
                o_ref[tile * FIELDS + f, 0:24, :] = v.astype(BF)
    for b in range(BANDS):
        for f in range(FIELDS):
            pair = [ends[8 * b : 8 * b + 8, (q * FIELDS + f) * 128 : (q * FIELDS + f + 1) * 128] for q in range(2)]
            o_ref[b * FIELDS + f, 24:40, :] = jnp.concatenate(pair, axis=0).astype(BF)


def ocean_kernel(
    f_ref, zt_ref, z_any, c_ref, o0_any, r_any, so_ref, co_ref,
    o_ref, w_ref, p_ref, h_ref, z_ref, r_ref, sem,
):
    lon = o_ref.shape[0]
    lev = position()[1]
    start = pl.multiple_of(lev * SLOTS, SLOTS)
    copies = [
        pltpu.make_async_copy(src, dst, sem.at[i])
        for i, (src, dst) in enumerate(((o0_any, o_ref), (r_any, r_ref), (z_any, z_ref)))
    ]
    for copy in copies:
        copy.start()
    copies[0].wait()
    copies[1].wait()
    lane_block = lax.broadcasted_iota(jnp.int32, (lon, 128), 1) // SLOTS

    def two_steps(j, _):
        pair = jnp.concatenate([f_ref[2 * j], f_ref[2 * j + 1]], axis=1)
        p_ref[...] = jnp.dot(zt_ref[...], pair, preferred_element_type=F32)
        for i in range(2):
            coarse = o_ref[...].astype(BF)
            pull = jnp.dot(
                jnp.concatenate([coarse, coarse], axis=1), c_ref[...], preferred_element_type=F32
            )
            updated = (o_ref[...] + (pull + p_ref[:, i * 128 : (i + 1) * 128])) * r_ref[...]
            o_ref[...] = updated
            k = 2 * j + i
            turned = pltpu.roll(updated, (k % 4 + FIELDS - lev) % FIELDS * SLOTS, 1)
            w_ref[k // 4] = jnp.where(lane_block == k % 4, turned, w_ref[k // 4])
        return 0

    lax.fori_loop(0, STEPS // 2, two_steps, 0)
    copies[2].wait()
    waves = jnp.concatenate([w_ref[q].astype(BF) for q in range(STEPS // 4)], axis=1)
    coef = jnp.dot(z_ref[...], waves, preferred_element_type=F32) * (1.0 / math.sqrt(lon))
    coef = jnp.concatenate([coef[:, q * 128 : (q + 1) * 128].T for q in range(STEPS // 4)], axis=0)
    co_ref[...] = jnp.dot(coef.astype(BF), join_columns(), preferred_element_type=F32).astype(BF)
    for x in range(0, lon, 128):
        w = min(128, lon - x)
        h_ref[:, 0:w] = o_ref[x : x + w, :].T
        so_ref[:, x : x + w] = h_ref[pl.ds(start, SLOTS), 0:w]


def unpack_kernel(b_any, o_ref, t_ref, v_ref, b_ref, sem):
    copy = pltpu.make_async_copy(b_any.at[:, 24:40, :], b_ref, sem)
    copy.start()
    copy.wait()

    def take(m, _):
        t_ref[pl.ds(pl.multiple_of(m * 16, 16), 16), :] = b_ref[m].astype(F32)
        return 0

    lax.fori_loop(0, WAVES, take, 0, unroll=8)
    for q in range(2):
        for h in range(8):
            v = t_ref[pl.ds(q * 8 + h, WAVES, stride=16), :].T
            for i in range(4 if q == 0 else 1):
                for c in range(2):
                    at = i * 32 + c * LEVELS
                    v_ref[c, pl.ds((4 * q + i) * 8 + h, LEVELS, stride=LAT), :] = v[at : at + LEVELS]
    both = jnp.concatenate([v_ref[0], v_ref[1]], axis=1).astype(BF)
    o_ref[...] = jnp.dot(both, join_columns(), preferred_element_type=F32)


def vmem(n):
    return [pl.BlockSpec(memory_space=pltpu.VMEM)] * n


def anywhere(n):
    return [pl.BlockSpec(memory_space=pl.ANY)] * n


def smem(n):
    return [pl.BlockSpec(memory_space=pltpu.SMEM)] * n


def call(kernel, in_specs, out_shape, scratch):
    return pl.pallas_call(
        kernel,
        out_shape=out_shape,
        in_specs=in_specs,
        out_specs=jax.tree.map(lambda _: pl.BlockSpec(memory_space=pltpu.VMEM), out_shape),
        scratch_shapes=scratch,
    )


def shape(dims, kind):
    return jax.ShapeDtypeStruct(dims, kind)


def state_selection():
    col = jnp.arange(FIELDS * 128, dtype=jnp.int32)[None, :]
    row = jnp.arange(ITEMS * 8, dtype=jnp.int32)[:, None]
    item = row // 8
    same = (col % ITEMS == item) & (col // 128 == row % 8 // 2)
    same_c = (col % 64 // ITEMS == row % 2) | (item == 28) | (item == 29)
    return jnp.stack([same & same_c & (col % 128 // 64 == q) for q in range(2)]).astype(BF)


def end_selection():
    row = jnp.arange(LO * 128, dtype=jnp.int32)[:, None]
    col = jnp.arange(2 * FIELDS * 128, dtype=jnp.int32)[None, :]
    lo = col // 512 * 4 + col % 128 // 32
    at = lo * 128 + col % LEVELS * 8 + col % 512 // 128 * 2 + col % 32 // LEVELS
    return (row == at).astype(BF)


def per_device(
    air_fourier_coefficients,
    quadrature_factor,
    associated_polynomial_table,
    east_west_harmonic,
    boundary_diffusion,
    bulk_transfer_coefficient,
    skin_heat_earlier,
    sea_boundary_values,
    sea_damping_speed,
    sea_coupling_matrix,
    patch_active_entries,
    sea_southern_parallel,
    sea_northern_share,
    air_paired_cells,
    air_second_share,
):
    band = lax.axis_index("band")
    lon = sea_boundary_values.shape[2]
    degree_count = associated_polynomial_table.shape[2]

    chunks = call(
        pack_kernel,
        smem(1) + vmem(8),
        shape((WAVES, CHUNK, 128), BF),
        [pltpu.VMEM((2, ITEMS * LAT, 128), F32), pltpu.VMEM((WAVES * XROWS, 128), F32)],
    )(
        patch_active_entries,
        air_fourier_coefficients.reshape(LEVELS * LAT, COLS),
        skin_heat_earlier.reshape(STEPS * LAT, COLS),
        boundary_diffusion.reshape(LEVELS * LEVELS, LAT),
        quadrature_factor[None],
        bulk_transfer_coefficient,
        sea_southern_parallel[None],
        sea_northern_share[None],
        jnp.asarray(pair_matrix(), BF),
    )
    got = lax.all_to_all(chunks, AXES, 0, 0, tiled=True)

    operator = call(
        operator_kernel,
        smem(1) + [pl.BlockSpec(memory_space=pl.ANY)],
        shape((NLAT, NLAT), BF),
        [
            pltpu.VMEM((LO, BANDS, 8, degree_count), BF),
            pltpu.VMEM((NLAT, degree_count), BF),
            pltpu.SemaphoreType.DMA((LO,)),
        ],
    )(east_west_harmonic, associated_polynomial_table.reshape(FIELDS, BANDS, LO, 8, degree_count))

    select_x = state_selection()
    select_end = end_selection()

    part = jnp.arange(160, dtype=jnp.int32)[:, None]
    longitude = jnp.where(part < 80, part % 40, part % 40 * 40)
    phases = longitude * east_west_harmonic[None, :] % lon
    angles = phases.astype(F32) * (2.0 * math.pi / lon)
    angle_parts = jnp.where(part // 40 % 2 == 0, jnp.cos(angles), jnp.sin(angles))
    own_sea, own_damp = sea_boundary_values[0], sea_damping_speed[0]
    sent = jnp.concatenate([own_sea.astype(BF), own_damp.astype(BF)], axis=0)
    others = []
    for d in range(1, FIELDS):
        others.append(lax.ppermute(sent, "lev", [(i, (i + d) % FIELDS) for i in range(FIELDS)]))
    zonal_t, zonal, ocean0, shrink, couple = call(
        tables_kernel,
        smem(1) + vmem(6),
        (
            shape((lon, COLS), BF),
            shape((COLS, lon), BF),
            shape((lon, 128), F32),
            shape((lon, 128), F32),
            shape((256, 128), BF),
        ),
        [pltpu.VMEM((lon, COLS), F32), pltpu.VMEM((2, 128, lon), F32)],
    )(sea_coupling_matrix, angle_parts, own_sea, own_damp, *others)

    got = got.reshape(BANDS, FIELDS, 5, 8, 128).transpose(2, 1, 0, 3, 4).reshape(5, FIELDS, 256, 128)
    partner = lax.ppermute(got[2:], "band", [(i, i ^ 1) for i in range(BANDS)])
    out = call(
        atmosphere_kernel,
        vmem(1) + anywhere(1) + vmem(1) + anywhere(2),
        shape((WAVES, OUT_ROWS, 128), BF),
        [
            pltpu.VMEM((NLAT // 128, NPAIR * 8, 128), F32),
            pltpu.VMEM((ITEMS * 8, NLAT), F32),
            pltpu.VMEM((LO, 128, 256), F32),
            pltpu.VMEM((2, 128, NLAT), BF),
            pltpu.VMEM((NLAT // 128, STEPS * 8, 128), F32),
            pltpu.VMEM((NLAT, BANDS * SLOTS), BF),
            pltpu.VMEM((3, FIELDS, 256, 128), BF),
            pltpu.VMEM((LO * 128, 1024), BF),
            pltpu.VMEM((NLAT, NLAT), BF),
            pltpu.SemaphoreType.DMA((3,)),
        ],
    )(got, partner, select_x, select_end, operator)

    back = lax.all_to_all(out, AXES, 0, 0, tiled=True)
    flux_in = back[:, :24].reshape(WAVES, 2, STEPS, 128).transpose(2, 1, 0, 3).reshape(STEPS, COLS, 128)
    sea_end, ocean_coef = call(
        ocean_kernel,
        vmem(2) + anywhere(1) + vmem(1) + anywhere(2),
        (shape((SLOTS, lon), F32), shape((STEPS * SLOTS, COLS), BF)),
        [
            pltpu.VMEM((lon, 128), F32),
            pltpu.VMEM((STEPS // 4, lon, 128), F32),
            pltpu.VMEM((lon, COLS), F32),
            pltpu.VMEM((128, 128), F32),
            pltpu.VMEM((COLS, lon), BF),
            pltpu.VMEM((lon, 128), F32),
            pltpu.SemaphoreType.DMA((3,)),
        ],
    )(flux_in, zonal_t, zonal, couple, ocean0, shrink)
    ocean_coef = ocean_coef.reshape(STEPS, SLOTS, COLS)
    air_coefficients_end = call(
        unpack_kernel,
        anywhere(1),
        shape((LEVELS * LAT, COLS), F32),
        [
            pltpu.VMEM((WAVES * 16, 128), F32),
            pltpu.VMEM((2, LEVELS * LAT, 128), F32),
            pltpu.VMEM((WAVES, 16, 128), BF),
            pltpu.SemaphoreType.DMA,
        ],
    )(back).reshape(1, LEVELS, LAT, COLS)

    up = [(i, i + 1) for i in range(BANDS - 1)]
    down = [(j, i) for i, j in up]
    before = lax.ppermute(ocean_coef, "band", up)
    after = lax.ppermute(ocean_coef, "band", down)
    neighbours = jnp.concatenate([before, ocean_coef, after], axis=1)
    slot_index = jnp.arange(3 * SLOTS, dtype=jnp.int32)[None, :]
    first = (air_paired_cells[0] - (band - 1) * SLOTS)[:, None]
    second = (air_paired_cells[1] - (band - 1) * SLOTS)[:, None]
    return_taps = jnp.where(slot_index == first, (1.0 - air_second_share)[:, None], 0.0) + jnp.where(
        slot_index == second, air_second_share[:, None], 0.0
    )
    skin_heat_newest = jnp.einsum(
        "ga,kac->kgc", return_taps.astype(BF), neighbours, preferred_element_type=F32
    )[:, None]
    return (air_coefficients_end, sea_end[None], skin_heat_newest)


def solution(mesh):
    return jax.shard_map(
        per_device,
        mesh=mesh,
        in_specs=(
            P("lev", None, "band", None),
            P("band"),
            P("band", None, None),
            P(),
            P("lev", None, None, "band"),
            P("lev", "band"),
            P(None, "lev", "band", None),
            P("lev", "band", None),
            P("lev", "band", None),
            P(),
            P("band"),
            P("band"),
            P("band"),
            P(None, "band"),
            P("band"),
        ),
        out_specs=(
            P("lev", None, "band", None),
            P("lev", "band", None),
            P(None, "lev", "band", None),
        ),
        check_vma=False,
    )
```
